256 devices in a mesh: grid: 128 (over x, z, y), rep: 2 (over core).
Axes of the slice: x: 4, y: 4, z: 8, core: 2. Of those that a mesh axis runs over, the one named last changes fastest.
Arguments:
- density_blocks: bfloat16 [3584, 4, 128, 128], P('grid'), may hold values from -0.046875 to 0.046875
- neighbours: int32 [3584, 4], P('grid'), may hold values from 0 to 3583, as said below
- relevant: int32 [3072, 8], P(('grid', 'rep')), may hold values from 0 to 3583, as said below
- batch_count: int32 [256], P(('grid', 'rep')), may hold values from 1 to 12, as said below
- basis_values: bfloat16 [3072, 8, 128, 128], P(('grid', 'rep')), may hold values from -6 to 6
- becke_weights: bfloat16 [3072, 128], P(('grid', 'rep')), may hold values from 0.0039978027 to 0.099609375
Outputs:
- xc_blocks: bfloat16 [3584, 4, 128, 128], P('grid')
The draws below stay inside these ranges and needn't reach their ends.
Inputs may be any that keep to these rules, and one draw needn't show every extreme that they name: neighbours[a, 0] = a; the 4 column groups of a row group are distinct and lie within 12 consecutive groups that contain a. `relevant`: the 8 groups of a batch are distinct and lie within 12 consecutive groups around a group owned by the batch's grid index; none lies more than 6 groups before the first or after the last group owned by that grid index. `batch_count`: some device has all 12 slots live in every draw.
All inputs are finite; a program needn't handle non-finite values.
Results may differ from the reference program's by a relative error of at most 0.0049.
Values may be sent and summed in bfloat16 or wider, within the bound.
A program may use at most 192 MiB of HBM per device.

```python
import math
import jax
import jax.numpy as jnp
from jax import lax

G = 128
NPT = 128
GROUPS_DEV = 28
K_BLOCKS = 4
R_GROUPS = 8
SPAN = 12
B_DEV = 12
GROUPS = 3584
BATCHES = 3072
N_GRID = 128
N_REP = 2


def permute_rows(key, count):
    keys = jax.random.split(key, count)

    def one_row(row_key):
        return jax.random.permutation(row_key, SPAN).astype(jnp.int32)
    return jax.vmap(one_row)(keys)


def draw_neighbours(key, part):
    row_ids = jnp.arange(GROUPS, dtype=jnp.int32)
    window_start = jnp.clip(row_ids - SPAN // 2, 0, GROUPS - SPAN)
    perms = permute_rows(jax.random.fold_in(key, 11), GROUPS)
    members = window_start[:, None] + perms
    positions = jnp.broadcast_to(jnp.arange(SPAN, dtype=jnp.int32)[None, :], members.shape)
    ranking = jnp.where(members == row_ids[:, None], -1, positions)
    order_ids = jnp.argsort(ranking, axis=1, stable=True)
    chosen = jnp.take_along_axis(members, order_ids, axis=1)
    return chosen[:, :K_BLOCKS].astype(jnp.int32)


def draw_relevant(key, part):
    batch_ids = jnp.arange(BATCHES, dtype=jnp.int32)
    owner_ids = batch_ids // (B_DEV * N_REP)
    offsets = jax.random.randint(jax.random.fold_in(key, 21), (BATCHES,), 0, GROUPS_DEV)
    centre = owner_ids * GROUPS_DEV + offsets
    window_start = jnp.clip(centre - SPAN // 2, 0, GROUPS - SPAN)
    perms = permute_rows(jax.random.fold_in(key, 23), BATCHES)
    members = window_start[:, None] + perms
    return members[:, :R_GROUPS].astype(jnp.int32)


def draw_batch_count(key, part):
    device_total = N_GRID * N_REP
    base_counts = jax.random.randint(jax.random.fold_in(key, 31), (device_total,), 1, B_DEV // 3 + 1)
    full_pick = jax.random.randint(jax.random.fold_in(key, 33), (device_total,), 0, 8) == 0
    forced = jax.random.randint(jax.random.fold_in(key, 35), (), 0, device_total)
    device_ids = jnp.arange(device_total, dtype=jnp.int32)
    return jnp.where(full_pick | (device_ids == forced), B_DEV, base_counts).astype(jnp.int32)


def steps_of(rng, extent, shards, least, top_value):
    def one(axis_at, shards_of):
        draws = jax.random.uniform(jax.random.fold_in(jax.random.fold_in(rng, 6), axis_at), (shards_of,), jnp.float32, least / len(shards), top_value / len(shards))
        return jnp.repeat(jnp.exp(draws), extent[axis_at] // shards_of).reshape((-1,) + (1,) * (len(extent) - axis_at - 1))

    factor_of = one(*shards[0])
    for cut in shards[1:]:
        factor_of = factor_of * one(*cut)
    return factor_of


def scatter_about(own_key, dims, scale, bound, pieces=(), kind=jnp.bfloat16):
    array = scale * jax.random.normal(own_key, dims, jnp.float32)
    if pieces:
        array = array * steps_of(own_key, dims, pieces, -0.22, 0.18)
    return jnp.clip(array, -bound, bound).astype(kind)


def setup_inputs(seed: int = 0) -> dict:
    streams_of = jax.random.split(jax.random.key(seed), 7)
    return {
        "density_blocks": scatter_about(streams_of[0], (GROUPS, K_BLOCKS, G, G), (G * G) ** -0.5, 0.046875, ((0, 128),)),
        "neighbours": draw_neighbours(jax.random.fold_in(streams_of[6], 71), 0),
        "relevant": draw_relevant(jax.random.fold_in(streams_of[6], 71), 0),
        "batch_count": draw_batch_count(jax.random.fold_in(streams_of[6], 71), 0),
        "basis_values": scatter_about(streams_of[4], (BATCHES, R_GROUPS, G, NPT), 1.0, 6.0, ((0, 256),)),
        "becke_weights": jnp.clip(jnp.exp(math.log(0.099609375) - 3.2155114 * jax.random.uniform(streams_of[5], (BATCHES, NPT), jnp.float32) ** steps_of(streams_of[5], (BATCHES, NPT), ((0, 256),), -0.2, 0.2)), 0.0039978027, 0.099609375).astype(jnp.bfloat16),
    }


slater_coef = 0.9847450218426965


def potential(density_at):
    return -slater_coef * density_at * (density_at * density_at + 1.0) ** (-1.0 / 3.0)


def batch_terms(slabs, slab_neighbours, groups, basis_vals, weight_row):
    matches = (slab_neighbours[:, :, None] == groups[None, None, :]).astype(jnp.float32)
    basis_wide = basis_vals.astype(jnp.float32)
    column_basis = jnp.einsum("ikj,jnp->iknp", matches, basis_wide).astype(jnp.bfloat16)
    spread = jnp.einsum("ikmn,iknp->imp", slabs.astype(jnp.float32), column_basis.astype(jnp.float32))
    density_at = jnp.sum(basis_wide * spread, axis=(0, 1))
    scaled = (basis_wide * (weight_row.astype(jnp.float32) * potential(density_at))[None, None, :]).astype(jnp.bfloat16)
    column_scaled = jnp.einsum("ikj,jnp->iknp", matches, scaled.astype(jnp.float32)).astype(jnp.bfloat16)
    return jnp.einsum("imp,iknp->ikmn", basis_wide, column_scaled.astype(jnp.float32))


def reference(density_blocks, neighbours, relevant, batch_count, basis_values, becke_weights):
    batch_total = relevant.shape[0]
    slot_ids = jnp.arange(batch_total, dtype=jnp.int32)
    live_flag = (slot_ids % B_DEV < batch_count[slot_ids // B_DEV]).astype(jnp.float32)

    def visit(total, item):
        groups, basis_vals, weight_row, flag = item
        blocks = batch_terms(density_blocks[groups], neighbours[groups], groups, basis_vals, weight_row) * flag
        return total.at[groups].add(blocks), None

    start_total = jnp.zeros(density_blocks.shape, jnp.float32)
    total, _ = lax.scan(visit, start_total, (relevant, basis_values, becke_weights, live_flag))
    return total.astype(jnp.bfloat16)
```

```python
import functools

import jax
import jax.numpy as jnp
from jax import lax
from jax.experimental import pallas as pl
from jax.experimental.pallas import tpu as pltpu
from jax.sharding import PartitionSpec as P

SPAN = 12
REACH = SPAN // 2
HALF = REACH // 2
MESH = pl.DeviceIdType.MESH
F32 = jnp.float32
BF16 = jnp.bfloat16

slater_coef = 0.9847450218426965


def potential(density_at):
    softened = jnp.exp(jnp.log(density_at * density_at + 1.0) * (-1.0 / 3.0))
    return -slater_coef * density_at * softened


def neighbours_of():
    count = lax.axis_size("grid")
    here = lax.axis_index("grid")
    left = lax.rem(here + count - 1, count)
    right = lax.rem(here + 1, count)
    return {"grid": left}, {"grid": right}, {"rep": 1 - lax.axis_index("rep")}


def meet(devices):
    barrier = pltpu.get_barrier_semaphore()
    for device in devices:
        pl.semaphore_signal(barrier, inc=1, device_id=device, device_id_type=MESH)
    pl.semaphore_wait(barrier, len(devices))


def remote(source, target, send_sem, recv_sem, device):
    return pltpu.make_async_remote_copy(
        src_ref=source,
        dst_ref=target,
        send_sem=send_sem,
        recv_sem=recv_sem,
        device_id=device,
        device_id_type=MESH,
    )


def halo_kernel(
    density, lists, low, high, lists_low, lists_high, send, recv, pass_send, pass_recv, list_send, list_recv
):
    left, right, partner = neighbours_of()
    first = lax.axis_index("rep") * HALF
    group_count = density.shape[0]
    meet((left, right, partner))
    list_copies = [
        remote(lists, lists_low, list_send.at[0], list_recv.at[0], right),
        remote(lists, lists_high, list_send.at[1], list_recv.at[1], left),
    ]
    for copy in list_copies:
        copy.start()
    moves = []
    for step in range(HALF):
        row = first + step
        for side, (source_row, target, device) in enumerate(
            ((group_count - REACH + row, low, right), (row, high, left))
        ):
            copy = remote(
                density.at[pl.ds(source_row, 1)],
                target.at[pl.ds(row, 1)],
                send.at[side, step],
                recv.at[side, step],
                device,
            )
            copy.start()
            relay = remote(
                target.at[pl.ds(row, 1)],
                target.at[pl.ds(row, 1)],
                pass_send.at[side, step],
                pass_recv.at[side, step],
                partner,
            )
            moves.append((copy, relay))
    for copy, relay in moves:
        copy.wait_recv()
        relay.start()
    for copy in list_copies:
        copy.wait()
    for copy, relay in moves:
        copy.wait_send()
        relay.wait()


def fetch_halo(density_blocks, neighbours):
    row_shape = density_blocks.shape[1:]
    edge = jax.ShapeDtypeStruct((REACH,) + row_shape, density_blocks.dtype)
    lists = jax.ShapeDtypeStruct(neighbours.shape, neighbours.dtype)
    anywhere = pl.BlockSpec(memory_space=pl.ANY)
    dma = pltpu.SemaphoreType.DMA
    return pl.pallas_call(
        halo_kernel,
        out_shape=(edge, edge, lists, lists),
        in_specs=[anywhere] * 2,
        out_specs=(anywhere,) * 4,
        scratch_shapes=[dma((2, HALF))] * 4 + [dma((2,))] * 2,
        compiler_params=pltpu.CompilerParams(collective_id=0, has_side_effects=True),
        name="halo",
    )(density_blocks, neighbours)


def batch_kernel(
    relevant, live, lists, lists_low, lists_high, weights, density, low, high, basis, partial,
    window, values, scaled, total, packed, place, window_sem, values_sem, out_sem,
):
    group_count, k_blocks = lists.shape
    batch_total, r_groups = relevant.shape
    rows = group_count + 2 * REACH
    base = lax.axis_index("grid") * group_count - REACH
    loads = [
        pltpu.make_async_copy(low, window.at[pl.ds(0, REACH)], window_sem.at[0]),
        pltpu.make_async_copy(high, window.at[pl.ds(REACH + group_count, REACH)], window_sem.at[1]),
        pltpu.make_async_copy(density, window.at[pl.ds(REACH, group_count)], window_sem.at[2]),
    ]

    def values_load(b):
        return pltpu.make_async_copy(basis.at[b], values.at[b, pl.ds(0, r_groups)], values_sem.at[b])

    values_load(0).start()
    for load in loads:
        load.start()
    for b in range(1, batch_total):
        values_load(b).start()

    blank = jnp.zeros(total.shape[2:], BF16)
    for slot in range(2):
        scaled[slot, r_groups] = blank

    def clear(row, carry):
        total[row] = jnp.zeros(total.shape[1:], F32)
        return carry

    lax.fori_loop(0, rows, clear, 0)

    def clear_blank(b, carry):
        values[b, r_groups] = blank
        return carry

    lax.fori_loop(0, batch_total, clear_blank, 0)
    for spot in range(place.shape[0]):
        place[spot] = -1
    for load in loads:
        load.wait()

    def column_group(row, k):
        at_low = row < REACH
        at_high = row >= REACH + group_count
        inner = lists[jnp.clip(row - REACH, 0, group_count - 1), k]
        below = lists_low[jnp.clip(group_count - REACH + row, 0, group_count - 1), k]
        above = lists_high[jnp.clip(row - REACH - group_count, 0, group_count - 1), k]
        return jnp.where(at_low, below, jnp.where(at_high, above, inner))

    def visit(b, carry):
        slot = lax.rem(b, 2)
        values_load(b).wait()
        local = [relevant[b, i] - base for i in range(r_groups)]
        for i in range(r_groups):
            place[local[i] + SPAN] = b * r_groups + i
        picks = []
        for i in range(r_groups):
            row_picks = []
            for k in range(k_blocks):
                stamp = place[column_group(local[i], k) - base + SPAN]
                found = lax.shift_right_arithmetic(stamp, 3) == b
                row_picks.append(jnp.where(found, stamp - b * r_groups, r_groups))
            picks.append(row_picks)
        density_at = jnp.zeros((8, window.shape[-1]), F32)
        for i in range(r_groups):
            spread = None
            for k in range(0, k_blocks, 2):
                left_side = jnp.concatenate([window[local[i], k], window[local[i], k + 1]], axis=1)
                right_side = jnp.concatenate(
                    [values[b, picks[i][k]], values[b, picks[i][k + 1]]], axis=0
                )
                term = jnp.dot(left_side, right_side, preferred_element_type=F32)
                spread = term if spread is None else spread + term
            product = values[b, i].astype(F32) * spread
            density_at = density_at + jnp.sum(product.reshape(-1, 8, product.shape[-1]), axis=0)
        density_row = jnp.sum(density_at, axis=0, keepdims=True)
        every_weight = weights[...].astype(F32)
        slots = lax.broadcasted_iota(jnp.int32, every_weight.shape, 0)
        weight_row = jnp.sum(jnp.where(slots == b, every_weight, 0.0), axis=0, keepdims=True)
        factor = weight_row * potential(density_row)
        for i in range(r_groups):
            scaled[slot, i] = (values[b, i].astype(F32) * factor).astype(BF16)
        for i in range(r_groups):
            for k in range(0, k_blocks, 2):
                columns = jnp.concatenate(
                    [scaled[slot, picks[i][k]], scaled[slot, picks[i][k + 1]]], axis=0
                )
                terms = lax.dot_general(
                    values[b, i], columns, (((1,), (1,)), ((), ())), preferred_element_type=F32
                )
                side = terms.shape[0]
                total[local[i], k] += terms[:, :side]
                total[local[i], k + 1] += terms[:, side:]
        return carry

    count = live[0]
    lax.fori_loop(0, count, visit, 0)

    def drain(b, carry):
        values_load(b).wait()
        return carry

    lax.fori_loop(count, batch_total, drain, 0)

    chunk = 4

    def out_copy(piece):
        rows_at = pl.ds(piece * chunk, chunk)
        return pltpu.make_async_copy(packed.at[rows_at], partial.at[rows_at], out_sem.at[piece])

    def pack(piece, carry):
        for step in range(chunk):
            packed[piece * chunk + step] = total[piece * chunk + step].astype(BF16)
        out_copy(piece).start()
        return carry

    lax.fori_loop(0, rows // chunk, pack, 0)

    def finish(piece, carry):
        out_copy(piece).wait()
        return carry

    lax.fori_loop(0, rows // chunk, finish, 0)


def partial_sums(relevant, batch_count, neighbours, halo, basis_values, becke_weights, density_blocks):
    low, high, lists_low, lists_high = halo
    group_count, k_blocks, side, _ = density_blocks.shape
    batch_total, r_groups = relevant.shape
    rows = group_count + 2 * REACH
    scalars = pl.BlockSpec(memory_space=pltpu.SMEM)
    vector = pl.BlockSpec(memory_space=pltpu.VMEM)
    anywhere = pl.BlockSpec(memory_space=pl.ANY)
    dma = pltpu.SemaphoreType.DMA
    return pl.pallas_call(
        batch_kernel,
        out_shape=jax.ShapeDtypeStruct((rows, k_blocks, side, side), BF16),
        in_specs=[scalars] * 5 + [vector] + [anywhere] * 4,
        out_specs=anywhere,
        scratch_shapes=[
            pltpu.VMEM((rows, k_blocks, side, side), BF16),
            pltpu.VMEM((batch_total, r_groups + 1, side, side), BF16),
            pltpu.VMEM((2, r_groups + 1, side, side), BF16),
            pltpu.VMEM((rows, k_blocks, side, side), F32),
            pltpu.VMEM((rows, k_blocks, side, side), BF16),
            pltpu.SMEM((rows + 2 * SPAN,), jnp.int32),
            dma((3,)),
            dma((batch_total,)),
            dma((rows // 4,)),
        ],
        name="batches",
    )(
        relevant, batch_count, neighbours, lists_low, lists_high, becke_weights,
        density_blocks, low, high, basis_values,
    )


def reduce_kernel(
    partial, out, got, mine, edge_out, edge_in,
    load_sem, swap_send, swap_recv, edge_send, edge_recv, done_send, done_recv,
):
    left, right, partner = neighbours_of()
    rep = lax.axis_index("rep")
    group_count = out.shape[0]
    inner = (group_count - 2 * REACH) // 2
    pieces = (
        (0, HALF, 0),
        (REACH + group_count, HALF, HALF),
        (REACH, HALF, 2 * HALF),
        (group_count, HALF, 3 * HALF),
        (2 * REACH, inner, 4 * HALF),
    )
    loads, swaps = [], []
    for index, (start, size, at) in enumerate(pieces):
        loads.append(
            pltpu.make_async_copy(
                partial.at[pl.ds(start + rep * size, size)], mine.at[pl.ds(at, size)], load_sem.at[index]
            )
        )
        swaps.append(
            remote(
                partial.at[pl.ds(start + (1 - rep) * size, size)],
                got.at[pl.ds(at, size)],
                swap_send.at[index],
                swap_recv.at[index],
                partner,
            )
        )
    for load in loads:
        load.start()
    meet((left, right, partner))
    for swap in swaps:
        swap.start()

    def joined(row):
        return mine[row].astype(F32) + got[row].astype(F32)

    def each_row(size, body):
        def step(row, carry):
            body(row)
            return carry

        lax.fori_loop(0, size, step, 0)

    edges = []
    for index, device, landing in ((0, left, HALF), (1, right, 0)):
        _, size, at = pieces[index]
        loads[index].wait()
        swaps[index].wait_recv()

        def add_edge(row, at=at):
            edge_out[at + row] = joined(at + row).astype(BF16)

        each_row(size, add_edge)
        copy = remote(
            edge_out.at[pl.ds(at, size)],
            edge_in.at[pl.ds(landing, size)],
            edge_send.at[index],
            edge_recv.at[1 - index],
            device,
        )
        copy.start()
        edges.append(copy)

    finals = []

    def hand_over(index, first, size):
        rows_at = pl.ds(first, size)
        copy = remote(
            out.at[rows_at], out.at[rows_at], done_send.at[index], done_recv.at[index], partner
        )
        copy.start()
        finals.append(copy)

    loads[4].wait()
    swaps[4].wait_recv()
    first_inner = REACH + rep * inner

    def add_inner(row):
        out[first_inner + row] = joined(4 * HALF + row).astype(BF16)

    each_row(inner, add_inner)
    hand_over(0, first_inner, inner)

    for index, edge, landing, owned in ((2, 1, 0, 0), (3, 0, HALF, group_count - REACH)):
        _, size, at = pieces[index]
        loads[index].wait()
        swaps[index].wait_recv()
        edges[edge].wait_send()
        pltpu.make_async_copy(
            edge_in.at[pl.ds(landing, size)], edge_in.at[pl.ds(landing, size)], edge_recv.at[landing // HALF]
        ).wait()
        first = owned + rep * size

        def add_owned(row, at=at, first=first, landing=landing):
            out[first + row] = (joined(at + row) + edge_in[landing + row].astype(F32)).astype(BF16)

        each_row(size, add_owned)
        hand_over(index - 1, first, size)
    for swap in swaps:
        swap.wait_send()
    for copy in finals:
        copy.wait()


def reduced(partial, group_count):
    rows, k_blocks, side, _ = partial.shape
    half_rows = rows // 2
    dma = pltpu.SemaphoreType.DMA
    return pl.pallas_call(
        reduce_kernel,
        out_shape=jax.ShapeDtypeStruct((group_count, k_blocks, side, side), BF16),
        in_specs=[pl.BlockSpec(memory_space=pl.ANY)],
        out_specs=pl.BlockSpec(memory_space=pltpu.VMEM),
        scratch_shapes=[
            pltpu.VMEM((half_rows, k_blocks, side, side), BF16),
            pltpu.VMEM((half_rows, k_blocks, side, side), BF16),
            pltpu.VMEM((REACH, k_blocks, side, side), BF16),
            pltpu.VMEM((REACH, k_blocks, side, side), BF16),
            dma((5,)),
            dma((5,)),
            dma((5,)),
            dma((2,)),
            dma((2,)),
            dma((3,)),
            dma((3,)),
        ],
        compiler_params=pltpu.CompilerParams(collective_id=1, has_side_effects=True),
        name="reduce",
    )(partial)


def shards(density_blocks, neighbours, relevant, batch_count, basis_values, becke_weights):
    halo = fetch_halo(density_blocks, neighbours)
    partial = partial_sums(
        relevant, batch_count, neighbours, halo, basis_values, becke_weights, density_blocks
    )
    return reduced(partial, density_blocks.shape[0])


def solution(mesh):
    placed = (
        P("grid", None, None, None),
        P("grid", None),
        P(("grid", "rep"), None),
        P(("grid", "rep")),
        P(("grid", "rep"), None, None, None),
        P(("grid", "rep"), None),
    )
    return jax.shard_map(
        shards, mesh=mesh, in_specs=placed, out_specs=P("grid", None, None, None), check_vma=False
    )
```

```python
import functools

import jax
import jax.numpy as jnp
from jax import lax
from jax.experimental import pallas as pl
from jax.experimental.pallas import tpu as pltpu
from jax.sharding import PartitionSpec as P

SPAN = 12
REACH = SPAN // 2
HALF = REACH // 2
MIB = 1 << 20
MESH = pl.DeviceIdType.MESH
F32 = jnp.float32
BF16 = jnp.bfloat16

slater_coef = 0.9847450218426965


def potential(density_at):
    softened = jnp.exp(jnp.log(density_at * density_at + 1.0) * (-1.0 / 3.0))
    return -slater_coef * density_at * softened


def surroundings():
    count = lax.axis_size("grid")
    here = lax.axis_index("grid")
    left = {"grid": jnp.maximum(here - 1, 0)}
    right = {"grid": jnp.minimum(here + 1, count - 1)}
    partner = {"rep": 1 - lax.axis_index("rep")}
    return (here > 0, left), (here < count - 1, right), partner


def meet(sides, partner):
    barrier = pltpu.get_barrier_semaphore()
    expected = 1
    for there, device in sides:

        @pl.when(there)
        def _():
            pl.semaphore_signal(barrier, inc=1, device_id=device, device_id_type=MESH)

        expected = expected + there.astype(jnp.int32)
    pl.semaphore_signal(barrier, inc=1, device_id=partner, device_id_type=MESH)
    pl.semaphore_wait(barrier, expected)


def remote(source, target, send_sem, recv_sem, device):
    return pltpu.make_async_remote_copy(
        src_ref=source,
        dst_ref=target,
        send_sem=send_sem,
        recv_sem=recv_sem,
        device_id=device,
        device_id_type=MESH,
    )


def each(size, body):
    def step(index, carry):
        body(index)
        return carry

    lax.fori_loop(0, size, step, 0)


def halo_kernel(
    density, lists, basis, window, values, total, lists_low, lists_high,
    local_sem, send, recv, pass_send, pass_recv, list_send, list_recv,
):
    (has_left, left), (has_right, right), partner = surroundings()
    first = lax.axis_index("rep") * HALF
    group_count = density.shape[0]
    batch_total, r_groups = basis.shape[:2]
    loads = [
        pltpu.make_async_copy(density, window.at[pl.ds(REACH, group_count)], local_sem.at[0]),
        pltpu.make_async_copy(basis, values.at[pl.ds(0, batch_total), pl.ds(0, r_groups)], local_sem.at[1]),
    ]
    for load in loads:
        load.start()
    meet(((has_left, left), (has_right, right)), partner)
    to_right, to_left = [], []
    for moves, has, device, own_row, at, list_at, side in (
        (to_right, has_right, right, group_count - REACH, 0, lists_low, 0),
        (to_left, has_left, left, 0, REACH + group_count, lists_high, 1),
    ):
        moves.append(remote(lists, list_at, list_send.at[side], list_recv.at[side], device))
        for step in range(HALF):
            row = first + step
            moves.append(
                remote(
                    density.at[pl.ds(own_row + row, 1)],
                    window.at[pl.ds(at + row, 1)],
                    send.at[side, step],
                    recv.at[side, step],
                    device,
                )
            )

        @pl.when(has)
        def _():
            for copy in moves:
                copy.start()

    def relays(at, side):
        return [
            remote(
                window.at[pl.ds(at + first + step, 1)],
                window.at[pl.ds(at + first + step, 1)],
                pass_send.at[side, step],
                pass_recv.at[side, step],
                partner,
            )
            for step in range(HALF)
        ]

    from_left = relays(0, 0)
    from_right = relays(REACH + group_count, 1)

    total[...] = jnp.zeros(total.shape, F32)

    def clear_blank(b):
        values[b, r_groups] = jnp.zeros(values.shape[2:], BF16)

    each(batch_total, clear_blank)

    for has, moves, passes in ((has_left, to_right, from_left), (has_right, to_left, from_right)):

        @pl.when(has)
        def _():
            moves[0].wait_recv()
            for copy, relay in zip(moves[1:], passes):
                copy.wait_recv()
                relay.start()

    for has, moves in ((has_right, to_right), (has_left, to_left)):

        @pl.when(has)
        def _():
            for copy in moves:
                copy.wait_send()

    for has, passes in ((has_left, from_left), (has_right, from_right)):

        @pl.when(has)
        def _():
            for relay in passes:
                relay.wait()

    for load in loads:
        load.wait()


def fetch_halo(density_blocks, lists, basis_values):
    group_count, k_blocks, side, _ = density_blocks.shape
    batch_total, r_groups = basis_values.shape[:2]
    rows = group_count + 2 * REACH
    list_shape = jax.ShapeDtypeStruct(lists.shape, lists.dtype)
    anywhere = pl.BlockSpec(memory_space=pl.ANY)
    in_hbm = pl.BlockSpec(memory_space=pltpu.HBM)
    vector = pl.BlockSpec(memory_space=pltpu.VMEM)
    dma = pltpu.SemaphoreType.DMA
    return pl.pallas_call(
        halo_kernel,
        out_shape=(
            pltpu.VMEM((rows, k_blocks, side, side), BF16),
            pltpu.VMEM((batch_total, r_groups + 1, side, side), BF16),
            pltpu.VMEM((rows, k_blocks, side, side), F32),
            list_shape,
            list_shape,
        ),
        in_specs=[in_hbm, anywhere, in_hbm],
        out_specs=(vector,) * 3 + (anywhere,) * 2,
        scratch_shapes=[dma((2,))] + [dma((2, HALF))] * 4 + [dma((2,))] * 2,
        compiler_params=pltpu.CompilerParams(
            collective_id=0, has_side_effects=True, vmem_limit_bytes=2 * MIB
        ),
        name="halo",
    )(
        pltpu.with_memory_space_constraint(density_blocks, pltpu.HBM),
        lists,
        pltpu.with_memory_space_constraint(basis_values, pltpu.HBM),
    )


def batch_kernel(
    relevant, live, lists, lists_low, lists_high, weights, window, values, start, total, scaled, place,
):
    del start
    k_blocks, group_count = lists.shape
    r_groups, _ = relevant.shape
    base = lax.axis_index("grid") * group_count - REACH
    blank = jnp.zeros(total.shape[2:], BF16)
    for slot in range(2):
        scaled[slot, r_groups] = blank
    for spot in range(place.shape[0]):
        place[spot] = -1

    def column_group(row, k):
        at_low = row < REACH
        at_high = row >= REACH + group_count
        inner = lists[k, jnp.clip(row - REACH, 0, group_count - 1)]
        below = lists_low[k, jnp.clip(group_count - REACH + row, 0, group_count - 1)]
        above = lists_high[k, jnp.clip(row - REACH - group_count, 0, group_count - 1)]
        return jnp.where(at_low, below, jnp.where(at_high, above, inner))

    def visit(b, carry):
        slot = lax.rem(b, 2)
        local = [relevant[i, b] - base for i in range(r_groups)]
        for i in range(r_groups):
            place[local[i] + SPAN] = b * r_groups + i
        picks = []
        for i in range(r_groups):
            row_picks = []
            for k in range(k_blocks):
                stamp = place[column_group(local[i], k) - base + SPAN]
                found = (stamp >= b * r_groups) & (stamp < (b + 1) * r_groups)
                row_picks.append(jnp.where(found, stamp - b * r_groups, r_groups))
            picks.append(row_picks)
        density_at = jnp.zeros((8, window.shape[-1]), F32)
        for i in range(r_groups):
            spread = None
            for k in range(0, k_blocks, 2):
                left_side = jnp.concatenate([window[local[i], k], window[local[i], k + 1]], axis=1)
                right_side = jnp.concatenate(
                    [values[b, picks[i][k]], values[b, picks[i][k + 1]]], axis=0
                )
                term = jnp.dot(left_side, right_side, preferred_element_type=F32)
                spread = term if spread is None else spread + term
            product = values[b, i].astype(F32) * spread
            density_at = density_at + jnp.sum(product.reshape(-1, 8, product.shape[-1]), axis=0)
        density_row = jnp.sum(density_at, axis=0, keepdims=True)
        every_weight = weights[...].astype(F32)
        slots = lax.broadcasted_iota(jnp.int32, every_weight.shape, 0)
        weight_row = jnp.sum(jnp.where(slots == b, every_weight, 0.0), axis=0, keepdims=True)
        factor = weight_row * potential(density_row)
        for i in range(r_groups):
            scaled[slot, i] = (values[b, i].astype(F32) * factor).astype(BF16)
        for i in range(r_groups):
            for k in range(0, k_blocks, 2):
                columns = jnp.concatenate(
                    [scaled[slot, picks[i][k]], scaled[slot, picks[i][k + 1]]], axis=0
                )
                terms = lax.dot_general(
                    values[b, i], columns, (((1,), (1,)), ((), ())), preferred_element_type=F32
                )
                side = terms.shape[0]
                total[local[i], k] += terms[:, :side]
                total[local[i], k + 1] += terms[:, side:]
        return carry

    lax.fori_loop(0, live[0], visit, 0)


def block_sums(relevant, batch_count, lists, fetched, becke_weights):
    window, values, start, lists_low, lists_high = fetched
    rows = window.shape[0]
    r_groups = relevant.shape[0]
    scalars = pl.BlockSpec(memory_space=pltpu.SMEM)
    vector = pl.BlockSpec(memory_space=pltpu.VMEM)
    return pl.pallas_call(
        batch_kernel,
        out_shape=pltpu.VMEM(start.shape, F32),
        in_specs=[scalars] * 5 + [vector] * 4,
        out_specs=vector,
        input_output_aliases={8: 0},
        scratch_shapes=[
            pltpu.VMEM((2, r_groups + 1) + window.shape[2:], BF16),
            pltpu.SMEM((rows + 2 * SPAN,), jnp.int32),
        ],
        compiler_params=pltpu.CompilerParams(vmem_limit_bytes=4 * MIB),
        name="batches",
    )(
        relevant, batch_count, lists, lists_low, lists_high, becke_weights,
        in_vmem(window), in_vmem(values), in_vmem(start),
    )


def in_vmem(array):
    return pltpu.with_memory_space_constraint(array, pltpu.VMEM)


def reduce_kernel(
    total, out, sent, got, edge_out, edge_in,
    swap_send, swap_recv, edge_send, edge_recv, done_send, done_recv,
):
    (has_left, left), (has_right, right), partner = surroundings()
    rep = lax.axis_index("rep")
    group_count = out.shape[0]
    inner = (group_count - 2 * REACH) // 2
    pieces = (
        (0, HALF, 0),
        (REACH + group_count, HALF, HALF),
        (REACH, HALF, 2 * HALF),
        (group_count, HALF, 3 * HALF),
        (2 * REACH, inner, 4 * HALF),
    )
    meet(((has_left, left), (has_right, right)), partner)
    swaps = []
    for index, (start, size, at) in enumerate(pieces):
        first = start + (1 - rep) * size

        def pack(row, at=at, first=first):
            sent[at + row] = total[first + row].astype(BF16)

        each(size, pack)
        rows_at = pl.ds(at, size)
        swap = remote(
            sent.at[rows_at], got.at[rows_at], swap_send.at[index], swap_recv.at[index], partner
        )
        swap.start()
        swaps.append(swap)

    def joined(index, row):
        start, size, at = pieces[index]
        return total[start + rep * size + row] + got[at + row].astype(F32)

    edges = []
    for index, has, device, landing in ((0, has_left, left, HALF), (1, has_right, right, 0)):
        _, size, at = pieces[index]
        swaps[index].wait_recv()

        def add_edge(row, index=index, at=at):
            edge_out[at + row] = joined(index, row).astype(BF16)

        each(size, add_edge)
        copy = remote(
            edge_out.at[pl.ds(at, size)],
            edge_in.at[pl.ds(landing, size)],
            edge_send.at[index],
            edge_recv.at[1 - index],
            device,
        )

        @pl.when(has)
        def _():
            copy.start()

        edges.append(copy)

    finals = []

    def hand_over(index, first, size):
        rows_at = pl.ds(first, size)
        copy = remote(
            out.at[rows_at], out.at[rows_at], done_send.at[index], done_recv.at[index], partner
        )
        copy.start()
        finals.append(copy)

    swaps[4].wait_recv()
    first_inner = REACH + rep * inner

    def add_inner(row):
        out[first_inner + row] = joined(4, row).astype(BF16)

    each(inner, add_inner)
    hand_over(0, first_inner, inner)

    for index, has, edge, landing, owned in (
        (2, has_left, 1, 0, 0),
        (3, has_right, 0, HALF, group_count - REACH),
    ):
        _, size, _ = pieces[index]
        swaps[index].wait_recv()
        first = owned + rep * size

        @pl.when(has)
        def _():
            edges[edge].wait_recv()

            def add_owned(row):
                arrived = edge_in[landing + row].astype(F32)
                out[first + row] = (joined(index, row) + arrived).astype(BF16)

            each(size, add_owned)

        @pl.when(jnp.logical_not(has))
        def _():
            def keep_owned(row):
                out[first + row] = joined(index, row).astype(BF16)

            each(size, keep_owned)

        hand_over(index - 1, first, size)
    for index, has in ((0, has_left), (1, has_right)):

        @pl.when(has)
        def _():
            edges[index].wait_send()

    for swap in swaps:
        swap.wait_send()
    for copy in finals:
        copy.wait()


def reduced(total, group_count):
    rows, k_blocks, side, _ = total.shape
    half_rows = rows // 2
    vector = pl.BlockSpec(memory_space=pltpu.VMEM)
    dma = pltpu.SemaphoreType.DMA
    return pl.pallas_call(
        reduce_kernel,
        out_shape=pltpu.VMEM((group_count, k_blocks, side, side), BF16),
        in_specs=[vector],
        out_specs=vector,
        scratch_shapes=[
            pltpu.VMEM((half_rows, k_blocks, side, side), BF16),
            pltpu.VMEM((half_rows, k_blocks, side, side), BF16),
            pltpu.VMEM((REACH, k_blocks, side, side), BF16),
            pltpu.VMEM((REACH, k_blocks, side, side), BF16),
            dma((5,)),
            dma((5,)),
            dma((2,)),
            dma((2,)),
            dma((3,)),
            dma((3,)),
        ],
        compiler_params=pltpu.CompilerParams(
            collective_id=1, has_side_effects=True, vmem_limit_bytes=12 * MIB
        ),
        name="reduce",
    )(in_vmem(total))


def shards(density_blocks, neighbours, relevant, batch_count, basis_values, becke_weights):
    lists = neighbours.T
    fetched = fetch_halo(density_blocks, lists, basis_values)
    total = block_sums(relevant.T, batch_count, lists, fetched, becke_weights)
    return reduced(total, density_blocks.shape[0])


def solution(mesh):
    placed = (
        P("grid", None, None, None),
        P("grid", None),
        P(("grid", "rep"), None),
        P(("grid", "rep")),
        P(("grid", "rep"), None, None, None),
        P(("grid", "rep"), None),
    )
    return jax.shard_map(
        shards, mesh=mesh, in_specs=placed, out_specs=P("grid", None, None, None), check_vma=False
    )
```

```python
import jax
import jax.numpy as jnp
from jax import lax
from jax.experimental import pallas as pl
from jax.experimental.pallas import tpu as pltpu
from jax.sharding import PartitionSpec as P

SPAN = 12
REACH = SPAN // 2
MIB = 1 << 20
MESH = pl.DeviceIdType.MESH
F32 = jnp.float32
BF16 = jnp.bfloat16

slater_coef = 0.9847450218426965


def potential(density_at):
    softened = jnp.exp(jnp.log(density_at * density_at + 1.0) * (-1.0 / 3.0))
    return -slater_coef * density_at * softened


def surroundings():
    count = lax.axis_size("grid")
    here = lax.axis_index("grid")
    rep = lax.axis_index("rep")
    there = here + 2 * rep - 1
    faces = (there >= 0) & (there < count)
    facing = {"grid": jnp.clip(there, 0, count - 1), "rep": 1 - rep}
    return rep, faces, facing, {"rep": 1 - rep}


def announce(faces, facing, partner):
    barrier = pltpu.get_barrier_semaphore()

    @pl.when(faces)
    def _():
        pl.semaphore_signal(barrier, inc=1, device_id=facing, device_id_type=MESH)

    pl.semaphore_signal(barrier, inc=1, device_id=partner, device_id_type=MESH)


def gather_round(faces):
    pl.semaphore_wait(pltpu.get_barrier_semaphore(), 1 + faces.astype(jnp.int32))


def remote(source, target, send_sem, recv_sem, device):
    return pltpu.make_async_remote_copy(
        src_ref=source,
        dst_ref=target,
        send_sem=send_sem,
        recv_sem=recv_sem,
        device_id=device,
        device_id_type=MESH,
    )


def each(size, body):
    def step(index, carry):
        body(index)
        return carry

    lax.fori_loop(0, size, step, 0)


def in_vmem(array):
    return pltpu.with_memory_space_constraint(array, pltpu.VMEM)


def in_hbm(array):
    return pltpu.with_memory_space_constraint(array, pltpu.HBM)


def spread_density(own, values, picks, rows, b):
    r_groups = len(rows)
    density_at = jnp.zeros((8, values.shape[-1]), F32)
    for i in range(r_groups):
        spread = None
        for k in range(0, len(picks[i]), 2):
            left_side = jnp.concatenate([own[rows[i], k], own[rows[i], k + 1]], axis=1)
            right_side = jnp.concatenate(
                [values[b, picks[i][k]], values[b, picks[i][k + 1]]], axis=0
            )
            term = jnp.dot(left_side, right_side, preferred_element_type=F32)
            spread = term if spread is None else spread + term
        product = values[b, i].astype(F32) * spread
        density_at = density_at + jnp.sum(product.reshape(-1, 8, product.shape[-1]), axis=0)
    return density_at


def halo_kernel(
    relevant, list_scalars, lists, density, basis, halo, values, total, density_out, table_out,
    own, edge_lists, table, table_scalars, edge_scalars,
    local_sem, small_sem, send, recv, pass_send, pass_recv, list_send, list_recv, lists_on_send, lists_on_recv,
):
    rep, faces, facing, partner = surroundings()
    group_count, k_blocks = density.shape[:2]
    batch_total, r_groups = basis.shape[:2]
    base = lax.axis_index("grid") * group_count
    load_own = pltpu.make_async_copy(density, own, local_sem.at[0])
    load_values = pltpu.make_async_copy(
        basis, values.at[pl.ds(0, batch_total), pl.ds(0, r_groups)], local_sem.at[1]
    )
    announce(faces, facing, partner)
    load_own.start()
    load_values.start()

    lanes = table.shape[1]
    lane = lax.broadcasted_iota(jnp.int32, (1, lanes), 1)
    batch_of = lax.shift_right_logical(lane, 3)
    spot = lane & (r_groups - 1)
    slots = []
    for j in range(r_groups):
        held = jnp.full((1, lanes), -1, jnp.int32)
        for b in range(batch_total):
            held = jnp.where(batch_of == b, relevant[j, b], held)
        slots.append(held)
    mine = slots[0]
    for j in range(1, r_groups):
        mine = jnp.where(spot == j, slots[j], mine)
    local = mine - base
    columns = []
    for k in range(k_blocks):
        held = jnp.full((1, lanes), -1, jnp.int32)
        for row in range(group_count):
            held = jnp.where(local == row, list_scalars[k, row], held)
        columns.append(held)

    def write_table(columns, rows):
        for k in range(k_blocks):
            pick = jnp.full((1, lanes), r_groups, jnp.int32)
            for j in range(r_groups):
                pick = jnp.where(columns[k] == slots[j], j, pick)
            table[k : k + 1, :] = pick
        table[k_blocks : k_blocks + 1, :] = rows

    table[...] = jnp.zeros(table.shape, jnp.int32)
    write_table(columns, jnp.clip(local, 0, group_count - 1))
    to_scalars = pltpu.make_async_copy(table, table_scalars, small_sem.at[0])
    to_scalars.start()

    gather_round(faces)
    list_pass = remote(edge_lists.at[rep], edge_lists.at[rep], lists_on_send, lists_on_recv, partner)
    moves, passes = [], []
    for step in range(REACH):
        at = pl.ds(rep * REACH + step, 1)
        far = pl.ds((1 - rep) * REACH + step, 1)
        source = density.at[pl.ds(rep * (group_count - REACH) + step, 1)]
        moves.append(remote(source, halo.at[far], send.at[step], recv.at[step], facing))
        passes.append(remote(halo.at[at], halo.at[at], pass_send.at[step], pass_recv.at[step], partner))
    list_move = remote(lists, edge_lists.at[1 - rep], list_send, list_recv, facing)

    @pl.when(faces)
    def _():
        list_move.start()
        for move in moves:
            move.start()

    total[...] = jnp.zeros(total.shape, F32)

    def clear_blank(b):
        values[b, r_groups] = jnp.zeros(values.shape[2:], BF16)

    each(batch_total, clear_blank)
    to_scalars.wait()
    load_own.wait()
    load_values.wait()

    def one_batch(b):
        picks = [
            [table_scalars[k, b * r_groups + i] for k in range(k_blocks)] for i in range(r_groups)
        ]
        rows = [table_scalars[k_blocks, b * r_groups + i] for i in range(r_groups)]
        density_out[b] = spread_density(own, values, picks, rows, b)

    each(batch_total, one_batch)

    @pl.when(faces)
    def _():
        list_move.wait_recv()
        list_pass.start()
        for move, onward in zip(moves, passes):
            move.wait_recv()
            onward.start()

    count = lax.axis_size("grid")
    other = lax.axis_index("grid") + 1 - 2 * rep
    other_faces = (other >= 0) & (other < count)

    @pl.when(other_faces)
    def _():
        list_pass.wait_recv()

    @pl.when(faces)
    def _():
        list_pass.wait_send()

    @pl.when(jnp.logical_not(faces))
    def _():
        edge_lists[rep] = jnp.full(edge_lists.shape[1:], -1, jnp.int32)

    @pl.when(jnp.logical_not(other_faces))
    def _():
        edge_lists[1 - rep] = jnp.full(edge_lists.shape[1:], -1, jnp.int32)

    lists_down = pltpu.make_async_copy(edge_lists, edge_scalars, small_sem.at[0])
    lists_down.start()
    lists_down.wait()
    for k in range(k_blocks):
        held = columns[k]
        for step in range(REACH):
            below = group_count - REACH + step
            held = jnp.where(local == step - REACH, edge_scalars[0, k, below], held)
            held = jnp.where(local == group_count + step, edge_scalars[1, k, step], held)
        columns[k] = held
    write_table(columns, local + REACH)
    table_out[...] = table[...]

    @pl.when(other_faces)
    def _():
        for onward in passes:
            onward.wait_recv()

    @pl.when(faces)
    def _():
        list_move.wait_send()
        for move, onward in zip(moves, passes):
            move.wait_send()
            onward.wait_send()


def fetch_halo(relevant, lists, density_blocks, basis_values):
    group_count, k_blocks, side, _ = density_blocks.shape
    batch_total, r_groups = basis_values.shape[:2]
    rows = group_count + 2 * REACH
    scalars = pl.BlockSpec(memory_space=pltpu.SMEM)
    vector = pl.BlockSpec(memory_space=pltpu.VMEM)
    main = pl.BlockSpec(memory_space=pltpu.HBM)
    dma = pltpu.SemaphoreType.DMA
    return pl.pallas_call(
        halo_kernel,
        out_shape=(
            pltpu.VMEM((2 * REACH, k_blocks, side, side), BF16),
            pltpu.VMEM((batch_total, r_groups + 1, side, side), BF16),
            pltpu.VMEM((rows, k_blocks, side, side), F32),
            pltpu.VMEM((batch_total, 8, side), F32),
            pltpu.VMEM((8, 128), jnp.int32),
        ),
        in_specs=[scalars, scalars, vector, main, main],
        out_specs=(vector,) * 5,
        scratch_shapes=[
            pltpu.VMEM((group_count, k_blocks, side, side), BF16),
            pltpu.VMEM((2,) + lists.shape, jnp.int32),
            pltpu.VMEM((8, 128), jnp.int32),
            pltpu.SMEM((8, 128), jnp.int32),
            pltpu.SMEM((2,) + lists.shape, jnp.int32),
            dma((2,)),
            dma((1,)),
            dma((REACH,)),
            dma((REACH,)),
            dma((REACH,)),
            dma((REACH,)),
            dma,
            dma,
            dma,
            dma,
        ],
        compiler_params=pltpu.CompilerParams(
            collective_id=0, has_side_effects=True, vmem_limit_bytes=8 * MIB
        ),
        name="halo",
    )(relevant, lists, lists, in_hbm(density_blocks), in_hbm(basis_values))


def batch_kernel(
    live, table, weights, halo, values, density_own, start, total,
    scaled_even, scaled_odd, density_at, factor, edge_list,
):
    del start
    batch_total, pages = values.shape[:2]
    r_groups = pages - 1
    k_blocks = total.shape[1]
    owned_end = total.shape[0] - REACH
    count = live[0]
    for scaled in (scaled_even, scaled_odd):
        scaled[r_groups] = jnp.zeros(total.shape[2:], BF16)
    density_at[...] = density_own[...]

    def collect(b, found):
        for i in range(r_groups):
            code = b * r_groups + i
            row = table[k_blocks, code]
            edge_list[found] = code
            outside = (row < REACH) | (row >= owned_end)
            found = found + outside.astype(jnp.int32)
        return found

    found = lax.fori_loop(0, count, collect, 0)
    edge_list[found] = 0

    def add_edges(step, carry):
        pieces = []
        for part in range(2):
            index = 2 * step + part
            code = edge_list[index]
            b = lax.shift_right_logical(code, 3)
            row = table[k_blocks, code]
            row = jnp.clip(jnp.where(row < REACH, row, row - owned_end + REACH), 0, 2 * REACH - 1)
            picks = [jnp.where(index < found, table[k, code], r_groups) for k in range(k_blocks)]
            spread = None
            for k in range(0, k_blocks, 2):
                left_side = jnp.concatenate([halo[row, k], halo[row, k + 1]], axis=1)
                right_side = jnp.concatenate([values[b, picks[k]], values[b, picks[k + 1]]], axis=0)
                term = jnp.dot(left_side, right_side, preferred_element_type=F32)
                spread = term if spread is None else spread + term
            product = values[b, code & (r_groups - 1)].astype(F32) * spread
            pieces.append((b, jnp.sum(product.reshape(-1, 8, product.shape[-1]), axis=0)))
        for b, piece in pieces:
            density_at[b] += piece
        return carry

    lax.fori_loop(0, lax.shift_right_logical(found + 1, 1), add_edges, 0)
    factor[...] = weights[...].astype(F32) * potential(jnp.sum(density_at[...], axis=1))

    def scale(b, scaled):
        row = factor[pl.ds(b, 1), :]
        for i in range(r_groups):
            scaled[i] = (values[b, i].astype(F32) * row).astype(BF16)

    def add_terms(b, scaled):
        for i in range(r_groups):
            code = b * r_groups + i
            row = table[k_blocks, code]
            for k in range(0, k_blocks, 2):
                columns = jnp.concatenate(
                    [scaled[table[k, code]], scaled[table[k + 1, code]]], axis=0
                )
                terms = lax.dot_general(
                    values[b, i], columns, (((1,), (1,)), ((), ())), preferred_element_type=F32
                )
                side = terms.shape[0]
                total[row, k] += terms[:, :side]
                total[row, k + 1] += terms[:, side:]

    def two(step, carry):
        scale(2 * step, scaled_even)
        scale(2 * step + 1, scaled_odd)
        add_terms(2 * step, scaled_even)
        add_terms(2 * step + 1, scaled_odd)
        return carry

    lax.fori_loop(0, lax.shift_right_logical(count, 1), two, 0)

    @pl.when((count & 1) == 1)
    def _():
        scale(count - 1, scaled_even)
        add_terms(count - 1, scaled_even)


def block_sums(batch_count, fetched, becke_weights):
    halo, values, start, density_own, table = fetched
    batch_total, pages, side, _ = values.shape
    scalars = pl.BlockSpec(memory_space=pltpu.SMEM)
    vector = pl.BlockSpec(memory_space=pltpu.VMEM)
    return pl.pallas_call(
        batch_kernel,
        out_shape=pltpu.VMEM(start.shape, F32),
        in_specs=[scalars] * 2 + [vector] * 5,
        out_specs=vector,
        input_output_aliases={6: 0},
        scratch_shapes=[
            pltpu.VMEM((pages, side, side), BF16),
            pltpu.VMEM((pages, side, side), BF16),
            pltpu.VMEM(density_own.shape, F32),
            pltpu.VMEM((batch_total, side), F32),
            pltpu.SMEM((128,), jnp.int32),
        ],
        compiler_params=pltpu.CompilerParams(vmem_limit_bytes=4 * MIB),
        name="batches",
    )(
        batch_count, table, becke_weights,
        in_vmem(halo), in_vmem(values), in_vmem(density_own), in_vmem(start),
    )


def reduce_kernel(
    total, out, sent, got, edge_out, edge_in,
    swap_send, swap_recv, edge_send, edge_recv, done_send, done_recv,
):
    rep, faces, facing, partner = surroundings()
    group_count = out.shape[0]
    inner = (group_count - 2 * REACH) // 2
    announce(faces, facing, partner)

    def halo_at(which):
        return which * (group_count + REACH)

    def edge_at(which):
        return REACH + which * (group_count - REACH)

    def inner_at(which):
        return 2 * REACH + which * inner

    def pack(first, at, size):
        def step(row):
            sent[at + row] = total[first + row].astype(BF16)

        each(size, step)

    swaps = []

    def swap(at, size):
        index = len(swaps)
        rows_at = pl.ds(at, size)
        copy = remote(
            sent.at[rows_at], got.at[rows_at], swap_send.at[index], swap_recv.at[index], partner
        )
        copy.start()
        swaps.append(copy)

    pack(halo_at(1 - rep), 0, REACH)
    gather_round(faces)
    for step in range(REACH):
        swap(step, 1)
    pack(inner_at(1 - rep), 2 * REACH, inner)
    swap(2 * REACH, inner)
    pack(edge_at(1 - rep), REACH, REACH)
    swap(REACH, REACH)

    edges = []
    for step in range(REACH):
        swaps[step].wait_recv()
        edge_out[step] = (total[halo_at(rep) + step] + got[step].astype(F32)).astype(BF16)
        edge = remote(edge_out.at[step], edge_in.at[step], edge_send.at[step], edge_recv.at[step], facing)
        edges.append(edge)

        @pl.when(faces)
        def _():
            edge.start()

    finals = []

    def hand_over(first, size):
        index = len(finals)
        rows_at = pl.ds(first, size)
        copy = remote(
            out.at[rows_at], out.at[rows_at], done_send.at[index], done_recv.at[index], partner
        )
        copy.start()
        finals.append(copy)

    swaps[REACH].wait_recv()
    first_inner = inner_at(rep)

    def add_inner(row):
        out[first_inner - REACH + row] = (
            total[first_inner + row] + got[2 * REACH + row].astype(F32)
        ).astype(BF16)

    each(inner, add_inner)
    hand_over(first_inner - REACH, inner)

    swaps[REACH + 1].wait_recv()
    for step in range(REACH):
        row = edge_at(rep) + step

        @pl.when(faces)
        def _():
            edges[step].wait_recv()
            out[row - REACH] = (
                total[row] + got[REACH + step].astype(F32) + edge_in[step].astype(F32)
            ).astype(BF16)

        @pl.when(jnp.logical_not(faces))
        def _():
            out[row - REACH] = (total[row] + got[REACH + step].astype(F32)).astype(BF16)

        hand_over(row - REACH, 1)

    @pl.when(faces)
    def _():
        for edge in edges:
            edge.wait_send()

    for copy in swaps:
        copy.wait_send()
    for copy in finals:
        copy.wait()


def reduced(total, group_count):
    rows, k_blocks, side, _ = total.shape
    half_rows = rows // 2
    vector = pl.BlockSpec(memory_space=pltpu.VMEM)
    dma = pltpu.SemaphoreType.DMA
    return pl.pallas_call(
        reduce_kernel,
        out_shape=pltpu.VMEM((group_count, k_blocks, side, side), BF16),
        in_specs=[vector],
        out_specs=vector,
        scratch_shapes=[
            pltpu.VMEM((half_rows, k_blocks, side, side), BF16),
            pltpu.VMEM((half_rows, k_blocks, side, side), BF16),
            pltpu.VMEM((REACH, k_blocks, side, side), BF16),
            pltpu.VMEM((REACH, k_blocks, side, side), BF16),
            dma((REACH + 2,)),
            dma((REACH + 2,)),
            dma((REACH,)),
            dma((REACH,)),
            dma((REACH + 1,)),
            dma((REACH + 1,)),
        ],
        compiler_params=pltpu.CompilerParams(
            collective_id=1, has_side_effects=True, vmem_limit_bytes=12 * MIB
        ),
        name="reduce",
    )(in_vmem(total))


def shards(density_blocks, neighbours, relevant, batch_count, basis_values, becke_weights):
    fetched = fetch_halo(relevant.T, neighbours.T, density_blocks, basis_values)
    total = block_sums(batch_count, fetched, becke_weights)
    return reduced(total, density_blocks.shape[0])


def solution(mesh):
    placed = (
        P("grid", None, None, None),
        P("grid", None),
        P(("grid", "rep"), None),
        P(("grid", "rep")),
        P(("grid", "rep"), None, None, None),
        P(("grid", "rep"), None),
    )
    return jax.shard_map(
        shards, mesh=mesh, in_specs=placed, out_specs=P("grid", None, None, None), check_vma=False
    )
```

```python
import functools

import jax
import jax.numpy as jnp
from jax import lax
from jax.experimental import pallas as pl
from jax.experimental.pallas import tpu as pltpu
from jax.sharding import PartitionSpec as P

SPAN = 12
REACH = SPAN // 2
MIB = 1 << 20
MESH = pl.DeviceIdType.MESH
F32 = jnp.float32
BF16 = jnp.bfloat16

slater_coef = 0.9847450218426965


def potential(density_at):
    softened = jnp.exp(jnp.log(density_at * density_at + 1.0) * (-1.0 / 3.0))
    return -slater_coef * density_at * softened


def surroundings():
    count = lax.axis_size("grid")
    here = lax.axis_index("grid")
    rep = lax.axis_index("rep")
    there = here + 2 * rep - 1
    faces = (there >= 0) & (there < count)
    facing = {"grid": jnp.clip(there, 0, count - 1), "rep": 1 - rep}
    return rep, faces, facing, {"rep": 1 - rep}


def announce(faces, facing, partner):
    barrier = pltpu.get_barrier_semaphore()

    @pl.when(faces)
    def _():
        pl.semaphore_signal(barrier, inc=1, device_id=facing, device_id_type=MESH)

    pl.semaphore_signal(barrier, inc=1, device_id=partner, device_id_type=MESH)


def gather_round(faces):
    pl.semaphore_wait(pltpu.get_barrier_semaphore(), 1 + faces.astype(jnp.int32))


def remote(source, target, send_sem, recv_sem, device):
    return pltpu.make_async_remote_copy(
        src_ref=source,
        dst_ref=target,
        send_sem=send_sem,
        recv_sem=recv_sem,
        device_id=device,
        device_id_type=MESH,
    )


def each(size, body):
    def step(index, carry):
        body(index)
        return carry

    lax.fori_loop(0, size, step, 0)


def in_vmem(array):
    return pltpu.with_memory_space_constraint(array, pltpu.VMEM)


def in_hbm(array):
    return pltpu.with_memory_space_constraint(array, pltpu.HBM)


def spread_density(own, values, picks, rows, b):
    r_groups = len(rows)
    density_at = jnp.zeros((8, values.shape[-1]), F32)
    for i in range(r_groups):
        spread = None
        for k in range(0, len(picks[i]), 2):
            left_side = jnp.concatenate([own[rows[i], k], own[rows[i], k + 1]], axis=1)
            right_side = jnp.concatenate(
                [values[b, picks[i][k]], values[b, picks[i][k + 1]]], axis=0
            )
            term = jnp.dot(left_side, right_side, preferred_element_type=F32)
            spread = term if spread is None else spread + term
        product = values[b, i].astype(F32) * spread
        density_at = density_at + jnp.sum(product.reshape(-1, 8, product.shape[-1]), axis=0)
    return density_at


def halo_kernel(
    relevant, lists, density, basis, halo, values, edge_total, density_out, table_out, sources,
    own, edge_lists, table, relevant_rows, relevant_scalars, list_scalars, table_scalars, edge_scalars,
    local_sem, small_sem, send, recv, pass_send, pass_recv, list_send, list_recv, lists_on_send, lists_on_recv,
):
    rep, faces, facing, partner = surroundings()
    group_count, k_blocks = density.shape[:2]
    batch_total, r_groups = basis.shape[:2]
    base = lax.axis_index("grid") * group_count
    announce(faces, facing, partner)
    small = [
        pltpu.make_async_copy(relevant, relevant_scalars, small_sem.at[0]),
        pltpu.make_async_copy(lists, list_scalars, small_sem.at[1]),
        pltpu.make_async_copy(relevant, relevant_rows, small_sem.at[2]),
    ]
    load_own = pltpu.make_async_copy(density, own, local_sem.at[0])
    load_values = pltpu.make_async_copy(
        basis, values.at[pl.ds(0, batch_total), pl.ds(0, r_groups)], local_sem.at[1]
    )
    for copy in small:
        copy.start()
    load_own.start()
    load_values.start()
    list_move = remote(lists, edge_lists.at[1 - rep], list_send, list_recv, facing)
    list_pass = remote(edge_lists.at[rep], edge_lists.at[rep], lists_on_send, lists_on_recv, partner)
    moves, passes = [], []
    for step in range(REACH):
        at = pl.ds(rep * REACH + step, 1)
        far = pl.ds((1 - rep) * REACH + step, 1)
        source = density.at[pl.ds(rep * (group_count - REACH) + step, 1)]
        moves.append(remote(source, halo.at[far], send.at[step], recv.at[step], facing))
        passes.append(remote(halo.at[at], halo.at[at], pass_send.at[step], pass_recv.at[step], partner))
    gather_round(faces)

    @pl.when(faces)
    def _():
        list_move.start()
        for move in moves:
            move.start()

    for copy in small:
        copy.wait()

    lanes = table.shape[1]
    lane = lax.broadcasted_iota(jnp.int32, (1, lanes), 1)
    batch_of = lax.shift_right_logical(lane, 3)
    spot = lane & (r_groups - 1)
    slots = []
    for j in range(r_groups):
        held = jnp.full((1, lanes), -1, jnp.int32)
        for b in range(batch_total):
            held = jnp.where(batch_of == b, relevant_scalars[j, b], held)
        slots.append(held)
    mine = slots[0]
    for j in range(1, r_groups):
        mine = jnp.where(spot == j, slots[j], mine)
    local = mine - base
    columns = []
    for k in range(k_blocks):
        held = jnp.full((1, lanes), -1, jnp.int32)
        for row in range(group_count):
            held = jnp.where(local == row, list_scalars[k, row], held)
        columns.append(held)

    def write_table(columns, rows):
        for k in range(k_blocks):
            pick = jnp.full((1, lanes), r_groups, jnp.int32)
            for j in range(r_groups):
                pick = jnp.where(columns[k] == slots[j], j, pick)
            table[k : k + 1, :] = pick
        table[k_blocks : k_blocks + 1, :] = rows

    table[...] = jnp.zeros(table.shape, jnp.int32)
    write_table(columns, jnp.clip(local, 0, group_count - 1))
    to_scalars = pltpu.make_async_copy(table, table_scalars, small_sem.at[0])
    to_scalars.start()

    owned_row = lax.broadcasted_iota(jnp.int32, sources.shape, 0)
    batch = lax.broadcasted_iota(jnp.int32, sources.shape, 1)
    found = jnp.full(sources.shape, batch_total * r_groups, jnp.int32)
    for j in range(r_groups):
        hit = relevant_rows[j : j + 1, :] - base == owned_row
        found = jnp.where(hit, batch * r_groups + j, found)
    sources[...] = found

    edge_total[...] = jnp.zeros(edge_total.shape, F32)

    def clear_blank(b):
        values[b, r_groups] = jnp.zeros(values.shape[2:], BF16)

    each(batch_total, clear_blank)
    to_scalars.wait()
    load_own.wait()
    load_values.wait()

    def one_batch(b):
        picks = [
            [table_scalars[k, b * r_groups + i] for k in range(k_blocks)] for i in range(r_groups)
        ]
        rows = [table_scalars[k_blocks, b * r_groups + i] for i in range(r_groups)]
        density_out[b] = spread_density(own, values, picks, rows, b)

    each(batch_total, one_batch)

    @pl.when(faces)
    def _():
        list_move.wait_recv()
        list_pass.start()
        for move, onward in zip(moves, passes):
            move.wait_recv()
            onward.start()

    count = lax.axis_size("grid")
    other = lax.axis_index("grid") + 1 - 2 * rep
    other_faces = (other >= 0) & (other < count)

    @pl.when(other_faces)
    def _():
        list_pass.wait_recv()

    @pl.when(faces)
    def _():
        list_pass.wait_send()

    @pl.when(jnp.logical_not(faces))
    def _():
        edge_lists[rep] = jnp.full(edge_lists.shape[1:], -1, jnp.int32)

    @pl.when(jnp.logical_not(other_faces))
    def _():
        edge_lists[1 - rep] = jnp.full(edge_lists.shape[1:], -1, jnp.int32)

    lists_down = pltpu.make_async_copy(edge_lists, edge_scalars, small_sem.at[1])
    lists_down.start()
    lists_down.wait()
    for k in range(k_blocks):
        held = columns[k]
        for step in range(REACH):
            below = group_count - REACH + step
            held = jnp.where(local == step - REACH, edge_scalars[0, k, below], held)
            held = jnp.where(local == group_count + step, edge_scalars[1, k, step], held)
        columns[k] = held
    write_table(columns, local + REACH)
    table_out[...] = table[...]

    @pl.when(other_faces)
    def _():
        for onward in passes:
            onward.wait_recv()

    @pl.when(faces)
    def _():
        list_move.wait_send()
        for move, onward in zip(moves, passes):
            move.wait_send()
            onward.wait_send()


def fetch_halo(relevant, lists, density_blocks, basis_values):
    group_count, k_blocks, side, _ = density_blocks.shape
    batch_total, r_groups = basis_values.shape[:2]
    vector = pl.BlockSpec(memory_space=pltpu.VMEM)
    main = pl.BlockSpec(memory_space=pltpu.HBM)
    dma = pltpu.SemaphoreType.DMA
    return pl.pallas_call(
        halo_kernel,
        out_shape=(
            pltpu.VMEM((2 * REACH, k_blocks, side, side), BF16),
            pltpu.VMEM((batch_total, r_groups + 1, side, side), BF16),
            pltpu.VMEM((2 * REACH, k_blocks, side, side), F32),
            pltpu.VMEM((batch_total, 8, side), F32),
            pltpu.VMEM((8, 128), jnp.int32),
            pltpu.VMEM((group_count, batch_total), jnp.int32),
        ),
        in_specs=[main] * 4,
        out_specs=(vector,) * 6,
        scratch_shapes=[
            pltpu.VMEM((group_count, k_blocks, side, side), BF16),
            pltpu.VMEM((2,) + lists.shape, jnp.int32),
            pltpu.VMEM((8, 128), jnp.int32),
            pltpu.VMEM(relevant.shape, jnp.int32),
            pltpu.SMEM(relevant.shape, jnp.int32),
            pltpu.SMEM(lists.shape, jnp.int32),
            pltpu.SMEM((8, 128), jnp.int32),
            pltpu.SMEM((2,) + lists.shape, jnp.int32),
            dma((2,)),
            dma((3,)),
            dma((REACH,)),
            dma((REACH,)),
            dma((REACH,)),
            dma((REACH,)),
            dma,
            dma,
            dma,
            dma,
        ],
        compiler_params=pltpu.CompilerParams(
            collective_id=0, has_side_effects=True, vmem_limit_bytes=8 * MIB
        ),
        name="halo",
    )(in_hbm(relevant), in_hbm(lists), in_hbm(density_blocks), in_hbm(basis_values))


def edge_kernel(
    group_count, live, table, weights, halo, values, density_own, start, edge_total, factor, density_at, edge_list,
):
    del start
    batch_total, pages = values.shape[:2]
    r_groups = pages - 1
    k_blocks = halo.shape[1]
    owned_end = REACH + group_count
    count = live[0]
    density_at[...] = density_own[...]

    def collect(b, found):
        for i in range(r_groups):
            code = b * r_groups + i
            row = table[k_blocks, code]
            edge_list[found] = code
            outside = (row < REACH) | (row >= owned_end)
            found = found + outside.astype(jnp.int32)
        return found

    found = lax.fori_loop(0, count, collect, 0)
    edge_list[found] = 0

    def entry(index):
        code = edge_list[index]
        row = table[k_blocks, code]
        row = jnp.clip(jnp.where(row < REACH, row, row - owned_end + REACH), 0, 2 * REACH - 1)
        picks = [jnp.where(index < found, table[k, code], r_groups) for k in range(k_blocks)]
        return lax.shift_right_logical(code, 3), code & (r_groups - 1), row, picks

    def two_of(body):
        def step(index, carry):
            body([entry(2 * index), entry(2 * index + 1)])
            return carry

        lax.fori_loop(0, lax.shift_right_logical(found + 1, 1), step, 0)

    def add_density(entries):
        parts = []
        for b, i, row, picks in entries:
            spread = None
            for k in range(0, k_blocks, 2):
                left_side = jnp.concatenate([halo[row, k], halo[row, k + 1]], axis=1)
                right_side = jnp.concatenate([values[b, picks[k]], values[b, picks[k + 1]]], axis=0)
                term = jnp.dot(left_side, right_side, preferred_element_type=F32)
                spread = term if spread is None else spread + term
            product = values[b, i].astype(F32) * spread
            parts.append(jnp.sum(product.reshape(-1, 8, product.shape[-1]), axis=0))
        for (b, _, _, _), part in zip(entries, parts):
            density_at[b] += part

    two_of(add_density)
    factors = weights[...].astype(F32) * potential(jnp.sum(density_at[...], axis=1))
    slot = lax.broadcasted_iota(jnp.int32, factors.shape, 0)
    factor[...] = jnp.where(slot < count, factors, 0.0)

    def add_terms(entries):
        terms = []
        for b, i, row, picks in entries:
            factor_row = factor[pl.ds(b, 1), :]
            for k in range(0, k_blocks, 2):
                columns = jnp.concatenate(
                    [(values[b, picks[k + n]].astype(F32) * factor_row).astype(BF16) for n in range(2)],
                    axis=0,
                )
                terms.append(
                    lax.dot_general(
                        values[b, i], columns, (((1,), (1,)), ((), ())), preferred_element_type=F32
                    )
                )
        side = halo.shape[-1]
        for (_, _, row, _), pair in zip(entries, (terms[: len(terms) // 2], terms[len(terms) // 2 :])):
            for k in range(k_blocks):
                edge_total[row, k] += pair[k // 2][:, side * (k % 2) : side * (k % 2 + 1)]

    two_of(add_terms)


def edge_sums(batch_count, fetched, becke_weights, group_count):
    halo, values, start, density_own, table, _ = fetched
    batch_total, _, side, _ = values.shape
    scalars = pl.BlockSpec(memory_space=pltpu.SMEM)
    vector = pl.BlockSpec(memory_space=pltpu.VMEM)
    return pl.pallas_call(
        functools.partial(edge_kernel, group_count),
        out_shape=(pltpu.VMEM(start.shape, F32), pltpu.VMEM((batch_total, side), F32)),
        in_specs=[scalars] * 2 + [vector] * 5,
        out_specs=(vector, vector),
        input_output_aliases={6: 0},
        scratch_shapes=[
            pltpu.VMEM(density_own.shape, F32),
            pltpu.SMEM((128,), jnp.int32),
        ],
        compiler_params=pltpu.CompilerParams(vmem_limit_bytes=4 * MIB),
        name="edges",
    )(
        batch_count, table, becke_weights,
        in_vmem(halo), in_vmem(values), in_vmem(density_own), in_vmem(start),
    )


def reduce_kernel(
    edge_total, values, factor, table, sources, out,
    table_scalars, source_scalars, terms, scaled_even, scaled_odd, sent, got, owned, edge_out, edge_in,
    small_sem, swap_send, swap_recv, edge_send, edge_recv, done_send, done_recv,
):
    rep, faces, facing, partner = surroundings()
    group_count, k_blocks = out.shape[:2]
    batch_total, pages = values.shape[:2]
    r_groups = pages - 1
    inner = (group_count - 2 * REACH) // 2
    announce(faces, facing, partner)
    small = [
        pltpu.make_async_copy(table, table_scalars, small_sem.at[0]),
        pltpu.make_async_copy(sources, source_scalars, small_sem.at[1]),
    ]
    for copy in small:
        copy.start()

    def edge_at(which):
        return which * (group_count - REACH)

    def inner_at(which):
        return REACH + which * inner

    swaps = []

    def swap(at, size):
        index = len(swaps)
        rows_at = pl.ds(at, size)
        copy = remote(
            sent.at[rows_at], got.at[rows_at], swap_send.at[index], swap_recv.at[index], partner
        )
        copy.start()
        swaps.append(copy)

    def pack_edge(row):
        sent[row] = edge_total[(1 - rep) * REACH + row].astype(BF16)

    each(REACH, pack_edge)
    gather_round(faces)
    for step in range(REACH):
        swap(step, 1)

    blank = jnp.zeros(values.shape[2:], BF16)
    for scaled in (scaled_even, scaled_odd):
        scaled[r_groups] = blank
    terms[batch_total * r_groups] = jnp.zeros(terms.shape[1:], F32)
    for copy in small:
        copy.wait()

    def scale(b, scaled):
        row = factor[pl.ds(b, 1), :]
        for i in range(r_groups):
            scaled[i] = (values[b, i].astype(F32) * row).astype(BF16)

    def make_terms(b, scaled):
        for i in range(r_groups):
            code = b * r_groups + i
            for k in range(0, k_blocks, 2):
                columns = jnp.concatenate(
                    [scaled[table_scalars[k, code]], scaled[table_scalars[k + 1, code]]], axis=0
                )
                pair = lax.dot_general(
                    values[b, i], columns, (((1,), (1,)), ((), ())), preferred_element_type=F32
                )
                side = pair.shape[0]
                terms[code, k] = pair[:, :side]
                terms[code, k + 1] = pair[:, side:]

    def two_batches(step):
        scale(2 * step, scaled_even)
        scale(2 * step + 1, scaled_odd)
        make_terms(2 * step, scaled_even)
        make_terms(2 * step + 1, scaled_odd)

    early = 1
    each(early, two_batches)

    edges = []
    for step in range(REACH):
        swaps[step].wait_recv()
        edge_out[step] = (edge_total[rep * REACH + step] + got[step].astype(F32)).astype(BF16)
        edge = remote(edge_out.at[step], edge_in.at[step], edge_send.at[step], edge_recv.at[step], facing)
        edges.append(edge)

        @pl.when(faces)
        def _():
            edge.start()

    each(batch_total // 2 - early, lambda step: two_batches(step + early))

    def row_sum(row, k):
        held = terms[source_scalars[row, 0], k]
        for b in range(1, batch_total):
            held = held + terms[source_scalars[row, b], k]
        return held

    def pack(first, at, size):
        def step(row):
            for k in range(k_blocks):
                sent[at + row, k] = row_sum(first + row, k).astype(BF16)

        each(size, step)
        swap(at, size)

    pack(inner_at(1 - rep), 2 * REACH, inner // 2)
    pack(inner_at(1 - rep) + inner // 2, 2 * REACH + inner // 2, inner // 2)
    pack(edge_at(1 - rep), REACH, REACH)

    finals = []

    def hand_over(first, size):
        index = len(finals)
        rows_at = pl.ds(first, size)
        copy = remote(
            out.at[rows_at], out.at[rows_at], done_send.at[index], done_recv.at[index], partner
        )
        copy.start()
        finals.append(copy)

    for half in range(2):
        swaps[REACH + half].wait_recv()
        first = inner_at(rep) + half * (inner // 2)
        at = 2 * REACH + half * (inner // 2)

        def add_inner(row, first=first, at=at):
            for k in range(k_blocks):
                out[first + row, k] = (row_sum(first + row, k) + got[at + row, k].astype(F32)).astype(BF16)

        each(inner // 2, add_inner)
        hand_over(first, inner // 2)

    swaps[REACH + 2].wait_recv()

    def add_owned(row):
        for k in range(k_blocks):
            owned[row, k] = row_sum(edge_at(rep) + row, k) + got[REACH + row, k].astype(F32)

    each(REACH, add_owned)
    for step in range(REACH):
        row = edge_at(rep) + step

        @pl.when(faces)
        def _():
            edges[step].wait_recv()
            out[row] = (owned[step] + edge_in[step].astype(F32)).astype(BF16)

        @pl.when(jnp.logical_not(faces))
        def _():
            out[row] = owned[step].astype(BF16)

        hand_over(row, 1)

    @pl.when(faces)
    def _():
        for edge in edges:
            edge.wait_send()

    for copy in swaps:
        copy.wait_send()
    for copy in finals:
        copy.wait()


def reduced(edge_total, factor, fetched):
    _, values, _, _, table, sources = fetched
    group_count = sources.shape[0]
    k_blocks, side, _ = edge_total.shape[1:]
    batch_total, pages = values.shape[:2]
    half_rows = (group_count + 2 * REACH) // 2
    vector = pl.BlockSpec(memory_space=pltpu.VMEM)
    dma = pltpu.SemaphoreType.DMA
    return pl.pallas_call(
        reduce_kernel,
        out_shape=pltpu.VMEM((group_count, k_blocks, side, side), BF16),
        in_specs=[vector] * 5,
        out_specs=vector,
        scratch_shapes=[
            pltpu.SMEM(table.shape, jnp.int32),
            pltpu.SMEM(sources.shape, jnp.int32),
            pltpu.VMEM((batch_total * (pages - 1) + 1, k_blocks, side, side), F32),
            pltpu.VMEM((pages, side, side), BF16),
            pltpu.VMEM((pages, side, side), BF16),
            pltpu.VMEM((half_rows, k_blocks, side, side), BF16),
            pltpu.VMEM((half_rows, k_blocks, side, side), BF16),
            pltpu.VMEM((REACH, k_blocks, side, side), F32),
            pltpu.VMEM((REACH, k_blocks, side, side), BF16),
            pltpu.VMEM((REACH, k_blocks, side, side), BF16),
            dma((2,)),
            dma((REACH + 3,)),
            dma((REACH + 3,)),
            dma((REACH,)),
            dma((REACH,)),
            dma((REACH + 2,)),
            dma((REACH + 2,)),
        ],
        compiler_params=pltpu.CompilerParams(
            collective_id=1, has_side_effects=True, vmem_limit_bytes=40 * MIB
        ),
        name="reduce",
    )(in_vmem(edge_total), in_vmem(values), in_vmem(factor), in_vmem(table), in_vmem(sources))


def shards(density_blocks, neighbours, relevant, batch_count, basis_values, becke_weights):
    fetched = fetch_halo(relevant.T, neighbours.T, density_blocks, basis_values)
    edge_total, factor = edge_sums(batch_count, fetched, becke_weights, density_blocks.shape[0])
    return reduced(edge_total, factor, fetched)


def solution(mesh):
    placed = (
        P("grid", None, None, None),
        P("grid", None),
        P(("grid", "rep"), None),
        P(("grid", "rep")),
        P(("grid", "rep"), None, None, None),
        P(("grid", "rep"), None),
    )
    return jax.shard_map(
        shards, mesh=mesh, in_specs=placed, out_specs=P("grid", None, None, None), check_vma=False
    )
```

```python
import functools

import jax
import jax.numpy as jnp
from jax import lax
from jax.experimental import pallas as pl
from jax.experimental.pallas import tpu as pltpu
from jax.sharding import PartitionSpec as P

SPAN = 12
REACH = SPAN // 2
MIB = 1 << 20
MESH = pl.DeviceIdType.MESH
F32 = jnp.float32
BF16 = jnp.bfloat16

slater_coef = 0.9847450218426965


def potential(density_at):
    softened = jnp.exp(jnp.log(density_at * density_at + 1.0) * (-1.0 / 3.0))
    return -slater_coef * density_at * softened


def surroundings():
    count = lax.axis_size("grid")
    here = lax.axis_index("grid")
    rep = lax.axis_index("rep")
    there = here + 2 * rep - 1
    faces = (there >= 0) & (there < count)
    facing = {"grid": jnp.clip(there, 0, count - 1), "rep": 1 - rep}
    return rep, faces, facing, {"rep": 1 - rep}


def announce(faces, facing, partner):
    barrier = pltpu.get_barrier_semaphore()

    @pl.when(faces)
    def _():
        pl.semaphore_signal(barrier, inc=1, device_id=facing, device_id_type=MESH)

    pl.semaphore_signal(barrier, inc=1, device_id=partner, device_id_type=MESH)


def gather_round(faces):
    pl.semaphore_wait(pltpu.get_barrier_semaphore(), 1 + faces.astype(jnp.int32))


def remote(source, target, send_sem, recv_sem, device):
    return pltpu.make_async_remote_copy(
        src_ref=source,
        dst_ref=target,
        send_sem=send_sem,
        recv_sem=recv_sem,
        device_id=device,
        device_id_type=MESH,
    )


def each(size, body):
    def step(index, carry):
        body(index)
        return carry

    lax.fori_loop(0, size, step, 0)


def in_vmem(array):
    return pltpu.with_memory_space_constraint(array, pltpu.VMEM)


def in_hbm(array):
    return pltpu.with_memory_space_constraint(array, pltpu.HBM)


def spread_density(own, values, picks, rows, b):
    r_groups = len(rows)
    density_at = jnp.zeros((8, values.shape[-1]), F32)
    for i in range(r_groups):
        spread = None
        for k in range(0, len(picks[i]), 2):
            left_side = jnp.concatenate([own[rows[i], k], own[rows[i], k + 1]], axis=1)
            right_side = jnp.concatenate(
                [values[b, picks[i][k]], values[b, picks[i][k + 1]]], axis=0
            )
            term = jnp.dot(left_side, right_side, preferred_element_type=F32)
            spread = term if spread is None else spread + term
        product = values[b, i].astype(F32) * spread
        density_at = density_at + jnp.sum(product.reshape(-1, 8, product.shape[-1]), axis=0)
    return density_at


def halo_kernel(
    live, relevant, lists, weights, density, basis,
    halo, values, edge_total, density_out, table_out, weights_out, sources,
    own, own_values, edge_lists, table, weights_in, relevant_rows, relevant_scalars, list_scalars, table_scalars, edge_scalars,
    local_sem, small_sem, send, recv, list_send, list_recv, lists_on_send, lists_on_recv, share_send, share_recv,
):
    rep, faces, facing, partner = surroundings()
    group_count, k_blocks = density.shape[:2]
    batch_total, r_groups = basis.shape[:2]
    base = lax.axis_index("grid") * group_count
    announce(faces, facing, partner)
    small = [
        pltpu.make_async_copy(relevant, relevant_scalars, small_sem.at[0]),
        pltpu.make_async_copy(lists, list_scalars, small_sem.at[1]),
        pltpu.make_async_copy(relevant, relevant_rows, small_sem.at[2]),
        pltpu.make_async_copy(weights, weights_in, small_sem.at[3]),
    ]
    mine_values = values.at[rep, pl.ds(0, batch_total), pl.ds(0, r_groups)]
    load_own = pltpu.make_async_copy(density, own, local_sem.at[0])
    load_values = pltpu.make_async_copy(
        basis, own_values.at[pl.ds(0, batch_total), pl.ds(0, r_groups)], local_sem.at[1]
    )
    keep_values = pltpu.make_async_copy(basis, mine_values, local_sem.at[2])
    for copy in small:
        copy.start()
    load_own.start()
    load_values.start()
    keep_values.start()
    list_move = remote(lists, edge_lists.at[1 - rep], list_send, list_recv, facing)
    list_pass = remote(edge_lists.at[rep], edge_lists.at[rep], lists_on_send, lists_on_recv, partner)
    moves = []
    for step in range(REACH):
        source = density.at[pl.ds(rep * (group_count - REACH) + step, 1)]
        moves.append(remote(source, halo.at[pl.ds(step, 1)], send.at[step], recv.at[step], facing))
    shares = [
        remote(source, target, share_send.at[index], share_recv.at[index], partner)
        for index, (source, target) in enumerate(
            (
                (basis, mine_values),
                (weights_out.at[rep], weights_out.at[rep]),
                (density_out.at[rep], density_out.at[rep]),
                (table_out.at[rep], table_out.at[rep]),
            )
        )
    ]
    gather_round(faces)

    @pl.when(faces)
    def _():
        list_move.start()
        for move in moves:
            move.start()

    shares[0].start()
    for copy in small:
        copy.wait()

    slot = lax.broadcasted_iota(jnp.int32, weights_in.shape, 0)
    weights_out[rep] = jnp.where(slot < live[0], weights_in[...].astype(F32), 0.0)
    shares[1].start()

    lanes = table.shape[1]
    lane = lax.broadcasted_iota(jnp.int32, (1, lanes), 1)
    batch_of = lax.shift_right_logical(lane, 3)
    spot = lane & (r_groups - 1)
    slots = []
    for j in range(r_groups):
        held = jnp.full((1, lanes), -1, jnp.int32)
        for b in range(batch_total):
            held = jnp.where(batch_of == b, relevant_scalars[j, b], held)
        slots.append(held)
    mine = slots[0]
    for j in range(1, r_groups):
        mine = jnp.where(spot == j, slots[j], mine)
    local = mine - base
    columns = []
    for k in range(k_blocks):
        held = jnp.full((1, lanes), -1, jnp.int32)
        for row in range(group_count):
            held = jnp.where(local == row, list_scalars[k, row], held)
        columns.append(held)

    def write_table(target, columns, rows):
        for k in range(k_blocks):
            pick = jnp.full((1, lanes), r_groups, jnp.int32)
            for j in range(r_groups):
                pick = jnp.where(columns[k] == slots[j], j, pick)
            target[k : k + 1, :] = pick
        target[k_blocks : k_blocks + 1, :] = rows
        target[k_blocks + 1 : k_blocks + 2, :] = jnp.full((1, lanes), live[0], jnp.int32)

    table[...] = jnp.zeros(table.shape, jnp.int32)
    write_table(table, columns, jnp.clip(local, 0, group_count - 1))
    to_scalars = pltpu.make_async_copy(table, table_scalars, small_sem.at[0])
    to_scalars.start()

    owned_row = lax.broadcasted_iota(jnp.int32, sources.shape, 0)
    batch = lax.broadcasted_iota(jnp.int32, sources.shape, 1)
    found = jnp.full(sources.shape, batch_total * r_groups, jnp.int32)
    for j in range(r_groups):
        hit = relevant_rows[j : j + 1, :] - base == owned_row
        found = jnp.where(hit, batch * r_groups + j, found)
    sources[...] = found

    edge_total[...] = jnp.zeros(edge_total.shape, F32)

    def clear_blank(b):
        blank = jnp.zeros(values.shape[3:], BF16)
        own_values[b, r_groups] = blank
        for core in range(2):
            values[core, b, r_groups] = blank

    each(batch_total, clear_blank)
    to_scalars.wait()
    load_own.wait()
    load_values.wait()

    def one_batch(b):
        picks = [
            [table_scalars[k, b * r_groups + i] for k in range(k_blocks)] for i in range(r_groups)
        ]
        rows = [table_scalars[k_blocks, b * r_groups + i] for i in range(r_groups)]
        density_out[rep, b] = spread_density(own, own_values, picks, rows, b)

    each(batch_total, one_batch)
    shares[2].start()

    count = lax.axis_size("grid")
    other = lax.axis_index("grid") + 1 - 2 * rep
    other_faces = (other >= 0) & (other < count)

    @pl.when(faces)
    def _():
        list_move.wait_recv()
        list_pass.start()

    @pl.when(other_faces)
    def _():
        list_pass.wait_recv()

    @pl.when(faces)
    def _():
        list_pass.wait_send()

    @pl.when(jnp.logical_not(faces))
    def _():
        edge_lists[rep] = jnp.full(edge_lists.shape[1:], -1, jnp.int32)

    @pl.when(jnp.logical_not(other_faces))
    def _():
        edge_lists[1 - rep] = jnp.full(edge_lists.shape[1:], -1, jnp.int32)

    lists_down = pltpu.make_async_copy(edge_lists, edge_scalars, small_sem.at[1])
    lists_down.start()
    lists_down.wait()
    for k in range(k_blocks):
        held = columns[k]
        for step in range(REACH):
            below = group_count - REACH + step
            held = jnp.where(local == step - REACH, edge_scalars[0, k, below], held)
            held = jnp.where(local == group_count + step, edge_scalars[1, k, step], held)
        columns[k] = held
    write_table(table_out.at[rep], columns, local + REACH)
    table_out[rep, k_blocks + 2 :, :] = jnp.zeros((8 - k_blocks - 2, lanes), jnp.int32)
    shares[3].start()

    @pl.when(faces)
    def _():
        for move in moves:
            move.wait_recv()
        list_move.wait_send()
        for move in moves:
            move.wait_send()

    keep_values.wait()
    for share in shares:
        share.wait()


def fetch_halo(live, relevant, lists, weights, density_blocks, basis_values):
    group_count, k_blocks, side, _ = density_blocks.shape
    batch_total, r_groups = basis_values.shape[:2]
    scalars = pl.BlockSpec(memory_space=pltpu.SMEM)
    vector = pl.BlockSpec(memory_space=pltpu.VMEM)
    main = pl.BlockSpec(memory_space=pltpu.HBM)
    dma = pltpu.SemaphoreType.DMA
    return pl.pallas_call(
        halo_kernel,
        out_shape=(
            pltpu.VMEM((REACH, k_blocks, side, side), BF16),
            pltpu.VMEM((2, batch_total, r_groups + 1, side, side), BF16),
            pltpu.VMEM((REACH, k_blocks, side, side), F32),
            pltpu.VMEM((2, batch_total, 8, side), F32),
            pltpu.VMEM((2, 8, 128), jnp.int32),
            pltpu.VMEM((2, batch_total, side), F32),
            pltpu.VMEM((group_count, batch_total), jnp.int32),
        ),
        in_specs=[scalars] + [main] * 5,
        out_specs=(vector,) * 7,
        scratch_shapes=[
            pltpu.VMEM((group_count, k_blocks, side, side), BF16),
            pltpu.VMEM((batch_total, r_groups + 1, side, side), BF16),
            pltpu.VMEM((2,) + lists.shape, jnp.int32),
            pltpu.VMEM((8, 128), jnp.int32),
            pltpu.VMEM(weights.shape, BF16),
            pltpu.VMEM(relevant.shape, jnp.int32),
            pltpu.SMEM(relevant.shape, jnp.int32),
            pltpu.SMEM(lists.shape, jnp.int32),
            pltpu.SMEM((8, 128), jnp.int32),
            pltpu.SMEM((2,) + lists.shape, jnp.int32),
            dma((3,)),
            dma((4,)),
            dma((REACH,)),
            dma((REACH,)),
            dma,
            dma,
            dma,
            dma,
            dma((4,)),
            dma((4,)),
        ],
        compiler_params=pltpu.CompilerParams(
            collective_id=0, has_side_effects=True, vmem_limit_bytes=10 * MIB
        ),
        name="halo",
    )(
        live, in_hbm(relevant), in_hbm(lists), in_hbm(weights),
        in_hbm(density_blocks), in_hbm(basis_values),
    )


def edge_kernel(
    group_count, table, weights, halo, values, density_owned, start, edge_sums, density, parts, edge_total,
    part_at, edge_list,
):
    batch_total, pages = values.shape[1:3]
    r_groups = pages - 1
    k_blocks = halo.shape[1]
    codes = batch_total * r_groups
    rep = lax.axis_index("rep")
    first = rep * (REACH + group_count)
    part_at[...] = jnp.zeros(part_at.shape, F32)
    del start

    found = 0
    for core in range(2):

        def collect(b, found):
            for i in range(r_groups):
                code = b * r_groups + i
                row = table[core, k_blocks, code] - first
                edge_list[found] = code + core * codes
                found = found + ((row >= 0) & (row < REACH)).astype(jnp.int32)
            return found

        found = lax.fori_loop(0, table[core, k_blocks + 1, 0], collect, found)
    edge_list[found] = 0

    def entry(index):
        listed = edge_list[index]
        core = (listed >= codes).astype(jnp.int32)
        code = listed - core * codes
        row = jnp.clip(table[core, k_blocks, code] - first, 0, REACH - 1)
        picks = [jnp.where(index < found, table[core, k, code], r_groups) for k in range(k_blocks)]
        return core, lax.shift_right_logical(code, 3), code & (r_groups - 1), row, picks

    def two_of(body):
        def step(index, carry):
            body([entry(2 * index), entry(2 * index + 1)])
            return carry

        lax.fori_loop(0, lax.shift_right_logical(found + 1, 1), step, 0)

    def add_density(entries):
        sums = []
        for core, b, i, row, picks in entries:
            spread = None
            for k in range(0, k_blocks, 2):
                left_side = jnp.concatenate([halo[row, k], halo[row, k + 1]], axis=1)
                right_side = jnp.concatenate(
                    [values[core, b, picks[k]], values[core, b, picks[k + 1]]], axis=0
                )
                term = jnp.dot(left_side, right_side, preferred_element_type=F32)
                spread = term if spread is None else spread + term
            product = values[core, b, i].astype(F32) * spread
            sums.append(jnp.sum(product.reshape(-1, 8, product.shape[-1]), axis=0))
        for (core, b, _, _, _), part in zip(entries, sums):
            part_at[core, b] += part

    two_of(add_density)
    for core in range(2):
        part = jnp.sum(part_at[core], axis=1)
        whole = jnp.sum(density_owned[core], axis=1) + part
        parts[core] = part
        density[core] = whole
    factor = part_at
    for core in range(2):
        scale = weights[core] * potential(density[core])
        factor[core] = jnp.broadcast_to(scale[:, None, :], factor.shape[1:])

    def add_terms(entries):
        terms = []
        for core, b, i, row, picks in entries:
            factor_row = factor[core, b, 0:1, :]
            for k in range(0, k_blocks, 2):
                columns = jnp.concatenate(
                    [
                        (values[core, b, picks[k + n]].astype(F32) * factor_row).astype(BF16)
                        for n in range(2)
                    ],
                    axis=0,
                )
                terms.append(
                    lax.dot_general(
                        values[core, b, i], columns, (((1,), (1,)), ((), ())), preferred_element_type=F32
                    )
                )
        side = halo.shape[-1]
        for n, (_, _, _, row, _) in enumerate(entries):
            for k in range(k_blocks):
                pair = terms[n * (k_blocks // 2) + k // 2]
                edge_total[row, k] += pair[:, side * (k % 2) : side * (k % 2 + 1)]

    two_of(add_terms)

    def pack(row):
        edge_sums[row] = edge_total[row].astype(BF16)

    each(REACH, pack)


def edge_work(fetched, group_count):
    halo, values, start, density_owned, table, weights, _ = fetched
    _, batch_total, _, side, _ = values.shape
    scalars = pl.BlockSpec(memory_space=pltpu.SMEM)
    vector = pl.BlockSpec(memory_space=pltpu.VMEM)
    rows = pltpu.VMEM((2, batch_total, side), F32)
    edge_sums, density, parts, _ = pl.pallas_call(
        functools.partial(edge_kernel, group_count),
        out_shape=(pltpu.VMEM(halo.shape, BF16), rows, rows, pltpu.VMEM(start.shape, F32)),
        in_specs=[scalars] + [vector] * 5,
        out_specs=(vector,) * 4,
        input_output_aliases={5: 3},
        scratch_shapes=[
            pltpu.VMEM(density_owned.shape, F32),
            pltpu.SMEM((256,), jnp.int32),
        ],
        compiler_params=pltpu.CompilerParams(vmem_limit_bytes=4 * MIB),
        name="edges",
    )(
        table, in_vmem(weights), in_vmem(halo), in_vmem(values), in_vmem(density_owned), in_vmem(start)
    )
    return edge_sums, density, parts


def reduce_kernel(
    edge_sums, density, parts, weights, values, table, sources, out,
    factor, table_scalars, source_scalars, terms, scaled_even, scaled_odd, sent, got, owned, edge_in, part_in,
    small_sem, swap_send, swap_recv, edge_send, edge_recv, done_send, done_recv, part_send, part_recv,
):
    rep, faces, facing, partner = surroundings()
    group_count, k_blocks = out.shape[:2]
    batch_total, pages = values.shape[1:3]
    r_groups = pages - 1
    inner = (group_count - 2 * REACH) // 2
    announce(faces, facing, partner)
    small = [
        pltpu.make_async_copy(table, table_scalars, small_sem.at[0]),
        pltpu.make_async_copy(sources, source_scalars, small_sem.at[1]),
    ]
    for copy in small:
        copy.start()
    blank = jnp.zeros(values.shape[3:], BF16)
    for scaled in (scaled_even, scaled_odd):
        scaled[r_groups] = blank
    terms[batch_total * r_groups] = jnp.zeros(terms.shape[1:], F32)
    edges = [
        remote(edge_sums.at[step], edge_in.at[step], edge_send.at[step], edge_recv.at[step], facing)
        for step in range(REACH)
    ]
    part_move = remote(parts.at[1 - rep], part_in, part_send, part_recv, partner)
    gather_round(faces)

    @pl.when(faces)
    def _():
        for edge in edges:
            edge.start()

    part_move.start()
    for copy in small:
        copy.wait()

    part_move.wait_recv()
    factor[...] = weights[rep] * potential(density[rep] + part_in[...])

    def edge_at(which):
        return which * (group_count - REACH)

    def inner_at(which):
        return REACH + which * inner

    def scale(b, scaled):
        row = factor[pl.ds(b, 1), :]
        for i in range(r_groups):
            scaled[i] = (values[rep, b, i].astype(F32) * row).astype(BF16)

    def make_terms(b, scaled):
        for i in range(r_groups):
            code = b * r_groups + i
            for k in range(0, k_blocks, 2):
                columns = jnp.concatenate(
                    [scaled[table_scalars[rep, k, code]], scaled[table_scalars[rep, k + 1, code]]], axis=0
                )
                pair = lax.dot_general(
                    values[rep, b, i], columns, (((1,), (1,)), ((), ())), preferred_element_type=F32
                )
                side = pair.shape[0]
                terms[code, k] = pair[:, :side]
                terms[code, k + 1] = pair[:, side:]

    def two_batches(step):
        scale(2 * step, scaled_even)
        scale(2 * step + 1, scaled_odd)
        make_terms(2 * step, scaled_even)
        make_terms(2 * step + 1, scaled_odd)

    each(batch_total // 2, two_batches)

    def row_sum(row, k):
        held = terms[source_scalars[row, 0], k]
        for b in range(1, batch_total):
            held = held + terms[source_scalars[row, b], k]
        return held

    swaps = []

    def pack(first, at, size):
        def step(row):
            for k in range(k_blocks):
                sent[at + row, k] = row_sum(first + row, k).astype(BF16)

        each(size, step)
        index = len(swaps)
        rows_at = pl.ds(at, size)
        copy = remote(
            sent.at[rows_at], got.at[rows_at], swap_send.at[index], swap_recv.at[index], partner
        )
        copy.start()
        swaps.append(copy)

    half_inner = inner // 2
    pack(inner_at(1 - rep), REACH, half_inner)
    pack(inner_at(1 - rep) + half_inner, REACH + half_inner, half_inner)
    pack(edge_at(1 - rep), 0, REACH)

    finals = []

    def hand_over(first, size):
        index = len(finals)
        rows_at = pl.ds(first, size)
        copy = remote(
            out.at[rows_at], out.at[rows_at], done_send.at[index], done_recv.at[index], partner
        )
        copy.start()
        finals.append(copy)

    for half in range(2):
        swaps[half].wait_recv()
        first = inner_at(rep) + half * half_inner
        at = REACH + half * half_inner

        def add_inner(row, first=first, at=at):
            for k in range(k_blocks):
                out[first + row, k] = (row_sum(first + row, k) + got[at + row, k].astype(F32)).astype(BF16)

        each(half_inner, add_inner)
        hand_over(first, half_inner)

    swaps[2].wait_recv()

    def add_owned(row):
        for k in range(k_blocks):
            owned[row, k] = row_sum(edge_at(rep) + row, k) + got[row, k].astype(F32)

    each(REACH, add_owned)
    for step in range(REACH):
        row = edge_at(rep) + step

        @pl.when(faces)
        def _():
            edges[step].wait_recv()
            out[row] = (owned[step] + edge_in[step].astype(F32)).astype(BF16)

        @pl.when(jnp.logical_not(faces))
        def _():
            out[row] = owned[step].astype(BF16)

        hand_over(row, 1)

    @pl.when(faces)
    def _():
        for edge in edges:
            edge.wait_send()

    part_move.wait_send()
    for copy in swaps:
        copy.wait_send()
    for copy in finals:
        copy.wait()


def reduced(edge_sums, density, parts, fetched):
    _, values, _, _, table, weights, sources = fetched
    group_count, batch_total = sources.shape
    k_blocks, side, _ = edge_sums.shape[1:]
    pages = values.shape[2]
    half_rows = group_count // 2
    vector = pl.BlockSpec(memory_space=pltpu.VMEM)
    dma = pltpu.SemaphoreType.DMA
    return pl.pallas_call(
        reduce_kernel,
        out_shape=pltpu.VMEM((group_count, k_blocks, side, side), BF16),
        in_specs=[vector] * 7,
        out_specs=vector,
        scratch_shapes=[
            pltpu.VMEM((batch_total, side), F32),
            pltpu.SMEM(table.shape, jnp.int32),
            pltpu.SMEM(sources.shape, jnp.int32),
            pltpu.VMEM((batch_total * (pages - 1) + 1, k_blocks, side, side), F32),
            pltpu.VMEM((pages, side, side), BF16),
            pltpu.VMEM((pages, side, side), BF16),
            pltpu.VMEM((half_rows, k_blocks, side, side), BF16),
            pltpu.VMEM((half_rows, k_blocks, side, side), BF16),
            pltpu.VMEM((REACH, k_blocks, side, side), F32),
            pltpu.VMEM((REACH, k_blocks, side, side), BF16),
            pltpu.VMEM((batch_total, side), F32),
            dma((2,)),
            dma((3,)),
            dma((3,)),
            dma((REACH,)),
            dma((REACH,)),
            dma((REACH + 2,)),
            dma((REACH + 2,)),
            dma,
            dma,
        ],
        compiler_params=pltpu.CompilerParams(
            collective_id=1, has_side_effects=True, vmem_limit_bytes=40 * MIB
        ),
        name="reduce",
    )(*[in_vmem(array) for array in (edge_sums, density, parts, weights, values, table, sources)])


def shards(density_blocks, neighbours, relevant, batch_count, basis_values, becke_weights):
    fetched = fetch_halo(
        batch_count, relevant.T, neighbours.T, becke_weights, density_blocks, basis_values
    )
    edge_sums, density, parts = edge_work(fetched, density_blocks.shape[0])
    return reduced(edge_sums, density, parts, fetched)


def solution(mesh):
    placed = (
        P("grid", None, None, None),
        P("grid", None),
        P(("grid", "rep"), None),
        P(("grid", "rep")),
        P(("grid", "rep"), None, None, None),
        P(("grid", "rep"), None),
    )
    return jax.shard_map(
        shards, mesh=mesh, in_specs=placed, out_specs=P("grid", None, None, None), check_vma=False
    )
```

```python
import jax
import jax.numpy as jnp
from jax import lax
from jax.experimental import pallas as pl
from jax.experimental.pallas import tpu as pltpu
from jax.sharding import PartitionSpec as P

SPAN = 12
REACH = SPAN // 2
MIB = 1 << 20
WIDE = 8
MESH = pl.DeviceIdType.MESH
F32 = jnp.float32
BF16 = jnp.bfloat16

slater_coef = 0.9847450218426965


def potential(density_at):
    softened = jnp.exp(jnp.log(density_at * density_at + 1.0) * (-1.0 / 3.0))
    return -slater_coef * density_at * softened


def surroundings():
    count = lax.axis_size("grid")
    here = lax.axis_index("grid")
    rep = lax.axis_index("rep")
    there = here + 2 * rep - 1
    faces = (there >= 0) & (there < count)
    facing = {"grid": jnp.clip(there, 0, count - 1), "rep": 1 - rep}
    return rep, faces, facing, {"rep": 1 - rep}


def announce(faces, facing, partner):
    barrier = pltpu.get_barrier_semaphore()

    @pl.when(faces)
    def _():
        pl.semaphore_signal(barrier, inc=1, device_id=facing, device_id_type=MESH)

    pl.semaphore_signal(barrier, inc=1, device_id=partner, device_id_type=MESH)


def gather_round(faces):
    pl.semaphore_wait(pltpu.get_barrier_semaphore(), 1 + faces.astype(jnp.int32))


def remote(source, target, send_sem, recv_sem, device):
    return pltpu.make_async_remote_copy(
        src_ref=source,
        dst_ref=target,
        send_sem=send_sem,
        recv_sem=recv_sem,
        device_id=device,
        device_id_type=MESH,
    )


def each(size, body):
    def step(index, carry):
        body(index)
        return carry

    lax.fori_loop(0, size, step, 0)


def in_vmem(array):
    return pltpu.with_memory_space_constraint(array, pltpu.VMEM)


def in_hbm(array):
    return pltpu.with_memory_space_constraint(array, pltpu.HBM)


def spread_density(own, values, picks, rows, b):
    r_groups = len(rows)
    density_at = jnp.zeros((8, values.shape[-1]), F32)
    for i in range(r_groups):
        spread = None
        for k in range(0, len(picks[i]), 2):
            left_side = jnp.concatenate([own[rows[i], k], own[rows[i], k + 1]], axis=1)
            right_side = jnp.concatenate(
                [values[b, picks[i][k]], values[b, picks[i][k + 1]]], axis=0
            )
            term = jnp.dot(left_side, right_side, preferred_element_type=F32)
            spread = term if spread is None else spread + term
        product = values[b, i].astype(F32) * spread
        density_at = density_at + jnp.sum(product.reshape(-1, 8, product.shape[-1]), axis=0)
    return density_at


def halo_kernel(
    live, relevant, lists, weights, density, basis,
    halo, values, edge_total, density_out, table_out, weights_out, sources,
    own, own_values, edge_lists, table, weights_in, relevant_rows, relevant_scalars, list_scalars, table_scalars, edge_scalars,
    local_sem, small_sem, send, recv, list_send, list_recv, lists_on_send, lists_on_recv, share_send, share_recv,
):
    rep, faces, facing, partner = surroundings()
    group_count, k_blocks = density.shape[:2]
    batch_total, r_groups = basis.shape[:2]
    base = lax.axis_index("grid") * group_count
    announce(faces, facing, partner)
    small = [
        pltpu.make_async_copy(relevant, relevant_scalars, small_sem.at[0]),
        pltpu.make_async_copy(lists, list_scalars, small_sem.at[1]),
        pltpu.make_async_copy(relevant, relevant_rows, small_sem.at[2]),
        pltpu.make_async_copy(weights, weights_in, small_sem.at[3]),
    ]
    mine_values = values.at[rep, pl.ds(0, batch_total), pl.ds(0, r_groups)]
    load_own = pltpu.make_async_copy(density, own, local_sem.at[0])
    load_values = pltpu.make_async_copy(
        basis, own_values.at[pl.ds(0, batch_total), pl.ds(0, r_groups)], local_sem.at[1]
    )
    keep_values = pltpu.make_async_copy(basis, mine_values, local_sem.at[2])
    for copy in small:
        copy.start()
    load_own.start()
    load_values.start()
    keep_values.start()
    list_move = remote(lists, edge_lists.at[1 - rep], list_send, list_recv, facing)
    list_pass = remote(edge_lists.at[rep], edge_lists.at[rep], lists_on_send, lists_on_recv, partner)
    moves = []
    for step in range(REACH):
        source = density.at[pl.ds(rep * (group_count - REACH) + step, 1)]
        moves.append(remote(source, halo.at[pl.ds(step, 1)], send.at[step], recv.at[step], facing))
    shares = [
        remote(source, target, share_send.at[index], share_recv.at[index], partner)
        for index, (source, target) in enumerate(
            (
                (basis, mine_values),
                (weights_out.at[rep], weights_out.at[rep]),
                (density_out.at[rep], density_out.at[rep]),
                (table_out.at[rep], table_out.at[rep]),
            )
        )
    ]
    gather_round(faces)

    @pl.when(faces)
    def _():
        list_move.start()
        for move in moves:
            move.start()

    shares[0].start()
    for copy in small:
        copy.wait()

    slot = lax.broadcasted_iota(jnp.int32, weights_in.shape, 0)
    weights_out[rep] = jnp.where(slot < live[0], weights_in[...].astype(F32), 0.0)
    shares[1].start()

    lanes = table.shape[1]
    lane = lax.broadcasted_iota(jnp.int32, (1, lanes), 1)
    batch_of = lax.shift_right_logical(lane, 3)
    spot = lane & (r_groups - 1)
    slots = []
    for j in range(r_groups):
        held = jnp.full((1, lanes), -1, jnp.int32)
        for b in range(batch_total):
            held = jnp.where(batch_of == b, relevant_scalars[j, b], held)
        slots.append(held)
    mine = slots[0]
    for j in range(1, r_groups):
        mine = jnp.where(spot == j, slots[j], mine)
    local = mine - base
    columns = []
    for k in range(k_blocks):
        held = jnp.full((1, lanes), -1, jnp.int32)
        for row in range(group_count):
            held = jnp.where(local == row, list_scalars[k, row], held)
        columns.append(held)

    in_use = lane < batch_total * r_groups

    def write_picks(target, columns):
        for k in range(k_blocks):
            pick = jnp.full((1, lanes), r_groups, jnp.int32)
            for j in range(r_groups):
                pick = jnp.where((columns[k] == slots[j]) & in_use, j, pick)
            target[k : k + 1, :] = pick

    table[...] = jnp.zeros(table.shape, jnp.int32)
    write_picks(table, columns)
    table[k_blocks : k_blocks + 1, :] = jnp.clip(local, 0, group_count - 1)
    to_scalars = pltpu.make_async_copy(table, table_scalars, small_sem.at[0])
    to_scalars.start()

    owned_row = lax.broadcasted_iota(jnp.int32, sources.shape, 0)
    batch = lax.broadcasted_iota(jnp.int32, sources.shape, 1)
    found = jnp.full(sources.shape, batch_total * r_groups, jnp.int32)
    for j in range(r_groups):
        hit = relevant_rows[j : j + 1, :] - base == owned_row
        found = jnp.where(hit, batch * r_groups + j, found)
    sources[...] = found

    edge_total[...] = jnp.zeros(edge_total.shape, F32)

    def clear_blank(b):
        blank = jnp.zeros(values.shape[3:], BF16)
        own_values[b, r_groups] = blank
        for core in range(2):
            values[core, b, r_groups] = blank

    each(batch_total, clear_blank)
    to_scalars.wait()
    load_own.wait()
    load_values.wait()

    def one_batch(b):
        picks = [
            [table_scalars[k, b * r_groups + i] for k in range(k_blocks)] for i in range(r_groups)
        ]
        rows = [table_scalars[k_blocks, b * r_groups + i] for i in range(r_groups)]
        density_out[rep, b] = spread_density(own, own_values, picks, rows, b)

    each(batch_total, one_batch)
    shares[2].start()

    count = lax.axis_size("grid")
    other = lax.axis_index("grid") + 1 - 2 * rep
    other_faces = (other >= 0) & (other < count)

    @pl.when(faces)
    def _():
        list_move.wait_recv()
        list_pass.start()

    @pl.when(other_faces)
    def _():
        list_pass.wait_recv()

    @pl.when(faces)
    def _():
        list_pass.wait_send()

    @pl.when(jnp.logical_not(faces))
    def _():
        edge_lists[rep] = jnp.full(edge_lists.shape[1:], -1, jnp.int32)

    @pl.when(jnp.logical_not(other_faces))
    def _():
        edge_lists[1 - rep] = jnp.full(edge_lists.shape[1:], -1, jnp.int32)

    lists_down = pltpu.make_async_copy(edge_lists, edge_scalars, small_sem.at[1])
    lists_down.start()
    lists_down.wait()
    for k in range(k_blocks):
        held = columns[k]
        for step in range(REACH):
            below = group_count - REACH + step
            held = jnp.where(local == step - REACH, edge_scalars[0, k, below], held)
            held = jnp.where(local == group_count + step, edge_scalars[1, k, step], held)
        columns[k] = held
    write_picks(table_out.at[rep], columns)
    below_row = jnp.where(local < 0, local + REACH, -1)
    above_row = jnp.where(local >= group_count, local - group_count, -1)
    table_out[rep, k_blocks : k_blocks + 1, :] = jnp.where(in_use, below_row, 0)
    table_out[rep, k_blocks + 1 : k_blocks + 2, :] = jnp.where(in_use, above_row, 0)
    table_out[rep, k_blocks + 2 : k_blocks + 3, :] = jnp.full((1, lanes), live[0], jnp.int32)
    table_out[rep, k_blocks + 3 :, :] = jnp.zeros((8 - k_blocks - 3, lanes), jnp.int32)
    shares[3].start()

    @pl.when(faces)
    def _():
        for move in moves:
            move.wait_recv()
        list_move.wait_send()
        for move in moves:
            move.wait_send()

    keep_values.wait()
    for share in shares:
        share.wait()


def fetch_halo(live, relevant, lists, weights, density_blocks, basis_values):
    group_count, k_blocks, side, _ = density_blocks.shape
    batch_total, r_groups = basis_values.shape[:2]
    scalars = pl.BlockSpec(memory_space=pltpu.SMEM)
    vector = pl.BlockSpec(memory_space=pltpu.VMEM)
    main = pl.BlockSpec(memory_space=pltpu.HBM)
    dma = pltpu.SemaphoreType.DMA
    return pl.pallas_call(
        halo_kernel,
        out_shape=(
            pltpu.VMEM((REACH, k_blocks, side, side), BF16),
            pltpu.VMEM((2, batch_total, r_groups + 1, side, side), BF16),
            pltpu.VMEM((REACH, k_blocks, side, side), F32),
            pltpu.VMEM((2, batch_total, 8, side), F32),
            pltpu.VMEM((2, 8, 128), jnp.int32),
            pltpu.VMEM((2, batch_total, side), F32),
            pltpu.VMEM((group_count, batch_total), jnp.int32),
        ),
        in_specs=[scalars] + [main] * 5,
        out_specs=(vector,) * 7,
        scratch_shapes=[
            pltpu.VMEM((group_count, k_blocks, side, side), BF16),
            pltpu.VMEM((batch_total, r_groups + 1, side, side), BF16),
            pltpu.VMEM((2,) + lists.shape, jnp.int32),
            pltpu.VMEM((8, 128), jnp.int32),
            pltpu.VMEM(weights.shape, BF16),
            pltpu.VMEM(relevant.shape, jnp.int32),
            pltpu.SMEM(relevant.shape, jnp.int32),
            pltpu.SMEM(lists.shape, jnp.int32),
            pltpu.SMEM((8, 128), jnp.int32),
            pltpu.SMEM((2,) + lists.shape, jnp.int32),
            dma((3,)),
            dma((4,)),
            dma((REACH,)),
            dma((REACH,)),
            dma,
            dma,
            dma,
            dma,
            dma((4,)),
            dma((4,)),
        ],
        compiler_params=pltpu.CompilerParams(
            collective_id=0, has_side_effects=True, vmem_limit_bytes=10 * MIB
        ),
        name="halo",
    )(
        live, in_hbm(relevant), in_hbm(lists), in_hbm(weights),
        in_hbm(density_blocks), in_hbm(basis_values),
    )


def edge_kernel(
    table, weights, halo, values, density_owned, start, edge_sums, density, parts, edge_total,
    part_at, edge_list,
):
    batch_total = density.shape[1]
    pages = values.shape[0] // (2 * batch_total)
    r_groups = pages - 1
    k_blocks = halo.shape[1]
    lanes = table.shape[2]
    side_row = k_blocks + lax.axis_index("rep")
    part_at[...] = jnp.zeros(part_at.shape, F32)
    del start

    found = 0
    for core in range(2):

        def collect(b, found):
            for i in range(r_groups):
                code = b * r_groups + i
                edge_list[found] = code + core * lanes
                found = found + (table[core, side_row, code] >= 0).astype(jnp.int32)
            return found

        found = lax.fori_loop(0, table[core, k_blocks + 2, 0], collect, found)
    edge_list[found] = batch_total * r_groups

    def entry(index):
        listed = edge_list[index]
        core = lax.shift_right_logical(listed, 7)
        code = listed & (lanes - 1)
        batch = core * batch_total + lax.shift_right_logical(code, 3)
        page = batch * pages
        picks = [page + table[core, k, code] for k in range(k_blocks)]
        return batch, page + (code & (r_groups - 1)), table[core, side_row, code], picks

    def for_entries(body):
        def wide(index, carry):
            body([entry(WIDE * index + n) for n in range(WIDE)])
            return carry

        wide_steps = lax.shift_right_logical(found, WIDE.bit_length() - 1)
        lax.fori_loop(0, wide_steps, wide, 0)

        def narrow(index, carry):
            body([entry(WIDE * wide_steps + 2 * index + n) for n in range(2)])
            return carry

        lax.fori_loop(0, lax.shift_right_logical(found - WIDE * wide_steps + 1, 1), narrow, 0)

    def add_density(entries):
        sums = []
        for batch, own_page, row, picks in entries:
            spread = None
            for k in range(0, k_blocks, 2):
                left_side = jnp.concatenate([halo[row, k], halo[row, k + 1]], axis=1)
                right_side = jnp.concatenate([values[picks[k]], values[picks[k + 1]]], axis=0)
                term = jnp.dot(left_side, right_side, preferred_element_type=F32)
                spread = term if spread is None else spread + term
            product = values[own_page].astype(F32) * spread
            sums.append(jnp.sum(product.reshape(-1, 8, product.shape[-1]), axis=0))
        for (batch, _, _, _), part in zip(entries, sums):
            part_at[batch] += part

    for_entries(add_density)
    factor = part_at
    for core in range(2):
        slots = pl.ds(core * batch_total, batch_total)
        part = jnp.sum(part_at[slots], axis=1)
        whole = jnp.sum(density_owned[core], axis=1) + part
        parts[core] = part
        density[core] = whole
        scale = weights[core] * potential(whole)
        factor[slots] = jnp.broadcast_to(scale[:, None, :], (batch_total,) + factor.shape[1:])

    def add_terms(entries):
        terms = []
        for batch, own_page, row, picks in entries:
            factor_row = factor[batch, 0:1, :]
            for k in range(0, k_blocks, 2):
                columns = jnp.concatenate(
                    [(values[picks[k + n]].astype(F32) * factor_row).astype(BF16) for n in range(2)],
                    axis=0,
                )
                terms.append(
                    lax.dot_general(
                        values[own_page], columns, (((1,), (1,)), ((), ())), preferred_element_type=F32
                    )
                )
        side = halo.shape[-1]
        for n, (_, _, row, _) in enumerate(entries):
            for k in range(k_blocks):
                pair = terms[n * (k_blocks // 2) + k // 2]
                edge_total[row, k] += pair[:, side * (k % 2) : side * (k % 2 + 1)]

    for_entries(add_terms)

    def pack(row):
        edge_sums[row] = edge_total[row].astype(BF16)

    each(REACH, pack)


def edge_work(fetched):
    halo, values, start, density_owned, table, weights, _ = fetched
    _, batch_total, pages, side, _ = values.shape
    flat = values.reshape(2 * batch_total * pages, side, side)
    scalars = pl.BlockSpec(memory_space=pltpu.SMEM)
    vector = pl.BlockSpec(memory_space=pltpu.VMEM)
    rows = pltpu.VMEM((2, batch_total, side), F32)
    edge_sums, density, parts, _ = pl.pallas_call(
        edge_kernel,
        out_shape=(pltpu.VMEM(halo.shape, BF16), rows, rows, pltpu.VMEM(start.shape, F32)),
        in_specs=[scalars] + [vector] * 5,
        out_specs=(vector,) * 4,
        input_output_aliases={5: 3},
        scratch_shapes=[
            pltpu.VMEM((2 * batch_total, 8, side), F32),
            pltpu.SMEM((256,), jnp.int32),
        ],
        compiler_params=pltpu.CompilerParams(vmem_limit_bytes=4 * MIB),
        name="edges",
    )(
        table, in_vmem(weights), in_vmem(halo), in_vmem(flat), in_vmem(density_owned), in_vmem(start)
    )
    return edge_sums, density, parts


def reduce_kernel(
    edge_sums, density, parts, weights, values, table, sources, out,
    factor, table_scalars, source_scalars, terms, scaled_even, scaled_odd, sent, got, owned, edge_in, part_in,
    small_sem, swap_send, swap_recv, edge_send, edge_recv, done_send, done_recv, part_send, part_recv,
):
    rep, faces, facing, partner = surroundings()
    group_count, k_blocks = out.shape[:2]
    batch_total, pages = values.shape[1:3]
    r_groups = pages - 1
    inner = (group_count - 2 * REACH) // 2
    announce(faces, facing, partner)
    small = [
        pltpu.make_async_copy(table, table_scalars, small_sem.at[0]),
        pltpu.make_async_copy(sources, source_scalars, small_sem.at[1]),
    ]
    for copy in small:
        copy.start()
    blank = jnp.zeros(values.shape[3:], BF16)
    for scaled in (scaled_even, scaled_odd):
        scaled[r_groups] = blank
    terms[batch_total * r_groups] = jnp.zeros(terms.shape[1:], F32)
    edges = [
        remote(edge_sums.at[step], edge_in.at[step], edge_send.at[step], edge_recv.at[step], facing)
        for step in range(REACH)
    ]
    part_move = remote(parts.at[1 - rep], part_in, part_send, part_recv, partner)
    gather_round(faces)

    @pl.when(faces)
    def _():
        for edge in edges:
            edge.start()

    part_move.start()
    for copy in small:
        copy.wait()

    part_move.wait_recv()
    factor[...] = weights[rep] * potential(density[rep] + part_in[...])

    def edge_at(which):
        return which * (group_count - REACH)

    def inner_at(which):
        return REACH + which * inner

    def scale(b, scaled):
        row = factor[pl.ds(b, 1), :]
        for i in range(r_groups):
            scaled[i] = (values[rep, b, i].astype(F32) * row).astype(BF16)

    def make_terms(b, scaled):
        for i in range(r_groups):
            code = b * r_groups + i
            for k in range(0, k_blocks, 2):
                columns = jnp.concatenate(
                    [scaled[table_scalars[rep, k, code]], scaled[table_scalars[rep, k + 1, code]]], axis=0
                )
                pair = lax.dot_general(
                    values[rep, b, i], columns, (((1,), (1,)), ((), ())), preferred_element_type=F32
                )
                side = pair.shape[0]
                terms[code, k] = pair[:, :side]
                terms[code, k + 1] = pair[:, side:]

    def two_batches(step):
        scale(2 * step, scaled_even)
        scale(2 * step + 1, scaled_odd)
        make_terms(2 * step, scaled_even)
        make_terms(2 * step + 1, scaled_odd)

    each(batch_total // 2, two_batches)

    def row_sum(row, k):
        held = terms[source_scalars[row, 0], k]
        for b in range(1, batch_total):
            held = held + terms[source_scalars[row, b], k]
        return held

    swaps = []

    def pack(first, at, size):
        def step(row):
            for k in range(k_blocks):
                sent[at + row, k] = row_sum(first + row, k).astype(BF16)

        each(size, step)
        index = len(swaps)
        rows_at = pl.ds(at, size)
        copy = remote(
            sent.at[rows_at], got.at[rows_at], swap_send.at[index], swap_recv.at[index], partner
        )
        copy.start()
        swaps.append(copy)

    half_inner = inner // 2
    pack(inner_at(1 - rep), REACH, half_inner)
    pack(inner_at(1 - rep) + half_inner, REACH + half_inner, half_inner)
    pack(edge_at(1 - rep), 0, REACH)

    finals = []

    def hand_over(first, size):
        index = len(finals)
        rows_at = pl.ds(first, size)
        copy = remote(
            out.at[rows_at], out.at[rows_at], done_send.at[index], done_recv.at[index], partner
        )
        copy.start()
        finals.append(copy)

    for half in range(2):
        swaps[half].wait_recv()
        first = inner_at(rep) + half * half_inner
        at = REACH + half * half_inner

        def add_inner(row, first=first, at=at):
            for k in range(k_blocks):
                out[first + row, k] = (row_sum(first + row, k) + got[at + row, k].astype(F32)).astype(BF16)

        each(half_inner, add_inner)
        hand_over(first, half_inner)

    swaps[2].wait_recv()

    def add_owned(row):
        for k in range(k_blocks):
            owned[row, k] = row_sum(edge_at(rep) + row, k) + got[row, k].astype(F32)

    each(REACH, add_owned)
    for step in range(REACH):
        row = edge_at(rep) + step

        @pl.when(faces)
        def _():
            edges[step].wait_recv()
            out[row] = (owned[step] + edge_in[step].astype(F32)).astype(BF16)

        @pl.when(jnp.logical_not(faces))
        def _():
            out[row] = owned[step].astype(BF16)

        hand_over(row, 1)

    @pl.when(faces)
    def _():
        for edge in edges:
            edge.wait_send()

    part_move.wait_send()
    for copy in swaps:
        copy.wait_send()
    for copy in finals:
        copy.wait()


def reduced(edge_sums, density, parts, fetched):
    _, values, _, _, table, weights, sources = fetched
    group_count, batch_total = sources.shape
    k_blocks, side, _ = edge_sums.shape[1:]
    pages = values.shape[2]
    half_rows = group_count // 2
    vector = pl.BlockSpec(memory_space=pltpu.VMEM)
    dma = pltpu.SemaphoreType.DMA
    return pl.pallas_call(
        reduce_kernel,
        out_shape=pltpu.VMEM((group_count, k_blocks, side, side), BF16),
        in_specs=[vector] * 7,
        out_specs=vector,
        scratch_shapes=[
            pltpu.VMEM((batch_total, side), F32),
            pltpu.SMEM(table.shape, jnp.int32),
            pltpu.SMEM(sources.shape, jnp.int32),
            pltpu.VMEM((batch_total * (pages - 1) + 1, k_blocks, side, side), F32),
            pltpu.VMEM((pages, side, side), BF16),
            pltpu.VMEM((pages, side, side), BF16),
            pltpu.VMEM((half_rows, k_blocks, side, side), BF16),
            pltpu.VMEM((half_rows, k_blocks, side, side), BF16),
            pltpu.VMEM((REACH, k_blocks, side, side), F32),
            pltpu.VMEM((REACH, k_blocks, side, side), BF16),
            pltpu.VMEM((batch_total, side), F32),
            dma((2,)),
            dma((3,)),
            dma((3,)),
            dma((REACH,)),
            dma((REACH,)),
            dma((REACH + 2,)),
            dma((REACH + 2,)),
            dma,
            dma,
        ],
        compiler_params=pltpu.CompilerParams(
            collective_id=1, has_side_effects=True, vmem_limit_bytes=40 * MIB
        ),
        name="reduce",
    )(*[in_vmem(array) for array in (edge_sums, density, parts, weights, values, table, sources)])


def shards(density_blocks, neighbours, relevant, batch_count, basis_values, becke_weights):
    fetched = fetch_halo(
        batch_count, relevant.T, neighbours.T, becke_weights, density_blocks, basis_values
    )
    edge_sums, density, parts = edge_work(fetched)
    return reduced(edge_sums, density, parts, fetched)


def solution(mesh):
    placed = (
        P("grid", None, None, None),
        P("grid", None),
        P(("grid", "rep"), None),
        P(("grid", "rep")),
        P(("grid", "rep"), None, None, None),
        P(("grid", "rep"), None),
    )
    return jax.shard_map(
        shards, mesh=mesh, in_specs=placed, out_specs=P("grid", None, None, None), check_vma=False
    )
```

```python
import jax
import jax.numpy as jnp
from jax import lax
from jax.experimental import pallas as pl
from jax.experimental.pallas import tpu as pltpu
from jax.sharding import PartitionSpec as P

SPAN = 12
REACH = SPAN // 2
MIB = 1 << 20
WIDE = 8
MESH = pl.DeviceIdType.MESH
F32 = jnp.float32
BF16 = jnp.bfloat16

slater_coef = 0.9847450218426965


def potential(density_at):
    softened = jnp.exp(jnp.log(density_at * density_at + 1.0) * (-1.0 / 3.0))
    return -slater_coef * density_at * softened


def surroundings():
    count = lax.axis_size("grid")
    here = lax.axis_index("grid")
    rep = lax.axis_index("rep")
    there = here + 2 * rep - 1
    faces = (there >= 0) & (there < count)
    facing = {"grid": jnp.clip(there, 0, count - 1), "rep": 1 - rep}
    return rep, faces, facing, {"rep": 1 - rep}


def announce(faces, facing, partner):
    barrier = pltpu.get_barrier_semaphore()

    @pl.when(faces)
    def _():
        pl.semaphore_signal(barrier, inc=1, device_id=facing, device_id_type=MESH)

    pl.semaphore_signal(barrier, inc=1, device_id=partner, device_id_type=MESH)


def gather_round(faces):
    pl.semaphore_wait(pltpu.get_barrier_semaphore(), 1 + faces.astype(jnp.int32))


def remote(source, target, send_sem, recv_sem, device):
    return pltpu.make_async_remote_copy(
        src_ref=source,
        dst_ref=target,
        send_sem=send_sem,
        recv_sem=recv_sem,
        device_id=device,
        device_id_type=MESH,
    )


def each(size, body):
    def step(index, carry):
        body(index)
        return carry

    lax.fori_loop(0, size, step, 0)


def in_vmem(array):
    return pltpu.with_memory_space_constraint(array, pltpu.VMEM)


def in_hbm(array):
    return pltpu.with_memory_space_constraint(array, pltpu.HBM)


def spread_density(own, values, picks, rows, b):
    r_groups = len(rows)
    density_at = jnp.zeros((8, values.shape[-1]), F32)
    for i in range(r_groups):
        spread = None
        for k in range(0, len(picks[i]), 2):
            left_side = jnp.concatenate([own[rows[i], k], own[rows[i], k + 1]], axis=1)
            right_side = jnp.concatenate(
                [values[b, picks[i][k]], values[b, picks[i][k + 1]]], axis=0
            )
            term = jnp.dot(left_side, right_side, preferred_element_type=F32)
            spread = term if spread is None else spread + term
        product = values[b, i].astype(F32) * spread
        density_at = density_at + jnp.sum(product.reshape(-1, 8, product.shape[-1]), axis=0)
    return density_at


def halo_kernel(
    live, relevant, lists, weights, density, basis,
    halo, values, edge_total, density_out, table_final, weights_out, sources,
    own, own_values, edge_lists, table, table_out, weights_in, relevant_rows, relevant_scalars, list_scalars, table_scalars, edge_scalars,
    local_sem, small_sem, send, recv, list_send, list_recv, lists_on_send, lists_on_recv, share_send, share_recv,
):
    rep, faces, facing, partner = surroundings()
    group_count, k_blocks = density.shape[:2]
    batch_total, r_groups = basis.shape[:2]
    base = lax.axis_index("grid") * group_count
    announce(faces, facing, partner)
    small = [
        pltpu.make_async_copy(relevant, relevant_scalars, small_sem.at[0]),
        pltpu.make_async_copy(lists, list_scalars, small_sem.at[1]),
        pltpu.make_async_copy(relevant, relevant_rows, small_sem.at[2]),
        pltpu.make_async_copy(weights, weights_in, small_sem.at[3]),
    ]
    mine_values = values.at[rep, pl.ds(0, batch_total), pl.ds(0, r_groups)]
    load_own = pltpu.make_async_copy(density, own, local_sem.at[0])
    load_values = pltpu.make_async_copy(
        basis, own_values.at[pl.ds(0, batch_total), pl.ds(0, r_groups)], local_sem.at[1]
    )
    keep_values = pltpu.make_async_copy(basis, mine_values, local_sem.at[2])
    for copy in small:
        copy.start()
    load_own.start()
    load_values.start()
    keep_values.start()
    list_move = remote(lists, edge_lists.at[1 - rep], list_send, list_recv, facing)
    list_pass = remote(edge_lists.at[rep], edge_lists.at[rep], lists_on_send, lists_on_recv, partner)
    moves = []
    for step in range(REACH):
        source = density.at[pl.ds(rep * (group_count - REACH) + step, 1)]
        moves.append(remote(source, halo.at[pl.ds(step, 1)], send.at[step], recv.at[step], facing))
    shares = [
        remote(source, target, share_send.at[index], share_recv.at[index], partner)
        for index, (source, target) in enumerate(
            (
                (basis, mine_values),
                (weights_out.at[rep], weights_out.at[rep]),
                (density_out.at[rep], density_out.at[rep]),
                (table_out.at[rep], table_out.at[rep]),
            )
        )
    ]
    gather_round(faces)

    @pl.when(faces)
    def _():
        list_move.start()
        for move in moves:
            move.start()

    shares[0].start()
    for copy in small:
        copy.wait()

    slot = lax.broadcasted_iota(jnp.int32, weights_in.shape, 0)
    weights_out[rep] = jnp.where(slot < live[0], weights_in[...].astype(F32), 0.0)
    shares[1].start()

    lanes = table.shape[1]
    lane = lax.broadcasted_iota(jnp.int32, (1, lanes), 1)
    batch_of = lax.shift_right_logical(lane, 3)
    spot = lane & (r_groups - 1)
    slots = []
    for j in range(r_groups):
        held = jnp.full((1, lanes), -1, jnp.int32)
        for b in range(batch_total):
            held = jnp.where(batch_of == b, relevant_scalars[j, b], held)
        slots.append(held)
    mine = slots[0]
    for j in range(1, r_groups):
        mine = jnp.where(spot == j, slots[j], mine)
    local = mine - base
    columns = []
    for k in range(k_blocks):
        held = jnp.full((1, lanes), -1, jnp.int32)
        for row in range(group_count):
            held = jnp.where(local == row, list_scalars[k, row], held)
        columns.append(held)

    in_use = lane < batch_total * r_groups

    def write_picks(target, columns):
        for k in range(k_blocks):
            pick = jnp.full((1, lanes), r_groups, jnp.int32)
            for j in range(r_groups):
                pick = jnp.where((columns[k] == slots[j]) & in_use, j, pick)
            target[k : k + 1, :] = pick

    table[...] = jnp.zeros(table.shape, jnp.int32)
    write_picks(table, columns)
    table[k_blocks : k_blocks + 1, :] = jnp.clip(local, 0, group_count - 1)
    to_scalars = pltpu.make_async_copy(table, table_scalars, small_sem.at[0])
    to_scalars.start()

    owned_row = lax.broadcasted_iota(jnp.int32, sources.shape, 0)
    batch = lax.broadcasted_iota(jnp.int32, sources.shape, 1)
    found = jnp.full(sources.shape, batch_total * r_groups, jnp.int32)
    for j in range(r_groups):
        hit = relevant_rows[j : j + 1, :] - base == owned_row
        found = jnp.where(hit, batch * r_groups + j, found)
    sources[...] = found

    edge_total[...] = jnp.zeros(edge_total.shape, F32)

    def clear_blank(b):
        blank = jnp.zeros(values.shape[3:], BF16)
        own_values[b, r_groups] = blank
        for core in range(2):
            values[core, b, r_groups] = blank

    each(batch_total, clear_blank)
    to_scalars.wait()
    load_own.wait()
    load_values.wait()

    def one_batch(b):
        picks = [
            [table_scalars[k, b * r_groups + i] for k in range(k_blocks)] for i in range(r_groups)
        ]
        rows = [table_scalars[k_blocks, b * r_groups + i] for i in range(r_groups)]
        density_out[rep, b] = spread_density(own, own_values, picks, rows, b)

    each(batch_total, one_batch)
    shares[2].start()

    count = lax.axis_size("grid")
    other = lax.axis_index("grid") + 1 - 2 * rep
    other_faces = (other >= 0) & (other < count)

    @pl.when(faces)
    def _():
        list_move.wait_recv()
        list_pass.start()

    @pl.when(other_faces)
    def _():
        list_pass.wait_recv()

    @pl.when(faces)
    def _():
        list_pass.wait_send()

    @pl.when(jnp.logical_not(faces))
    def _():
        edge_lists[rep] = jnp.full(edge_lists.shape[1:], -1, jnp.int32)

    @pl.when(jnp.logical_not(other_faces))
    def _():
        edge_lists[1 - rep] = jnp.full(edge_lists.shape[1:], -1, jnp.int32)

    lists_down = pltpu.make_async_copy(edge_lists, edge_scalars, small_sem.at[1])
    lists_down.start()
    lists_down.wait()
    for k in range(k_blocks):
        held = columns[k]
        for step in range(REACH):
            below = group_count - REACH + step
            held = jnp.where(local == step - REACH, edge_scalars[0, k, below], held)
            held = jnp.where(local == group_count + step, edge_scalars[1, k, step], held)
        columns[k] = held
    write_picks(table_out.at[rep], columns)
    below_row = jnp.where(local < 0, local + REACH, -1)
    above_row = jnp.where(local >= group_count, local - group_count, -1)
    table_out[rep, k_blocks : k_blocks + 1, :] = jnp.where(in_use, below_row, 0)
    table_out[rep, k_blocks + 1 : k_blocks + 2, :] = jnp.where(in_use, above_row, 0)
    table_out[rep, k_blocks + 2 : k_blocks + 3, :] = jnp.full((1, lanes), live[0], jnp.int32)
    table_out[rep, k_blocks + 3 :, :] = jnp.zeros((8 - k_blocks - 3, lanes), jnp.int32)
    shares[3].start()
    shares[3].wait()
    table_down = pltpu.make_async_copy(table_out, table_final, small_sem.at[0])
    table_down.start()
    table_down.wait()

    @pl.when(faces)
    def _():
        for move in moves:
            move.wait_recv()
        list_move.wait_send()
        for move in moves:
            move.wait_send()

    keep_values.wait()
    for share in shares[:3]:
        share.wait()


def fetch_halo(live, relevant, lists, weights, density_blocks, basis_values):
    group_count, k_blocks, side, _ = density_blocks.shape
    batch_total, r_groups = basis_values.shape[:2]
    scalars = pl.BlockSpec(memory_space=pltpu.SMEM)
    vector = pl.BlockSpec(memory_space=pltpu.VMEM)
    main = pl.BlockSpec(memory_space=pltpu.HBM)
    dma = pltpu.SemaphoreType.DMA
    return pl.pallas_call(
        halo_kernel,
        out_shape=(
            pltpu.VMEM((REACH, k_blocks, side, side), BF16),
            pltpu.VMEM((2, batch_total, r_groups + 1, side, side), BF16),
            pltpu.VMEM((REACH, k_blocks, side, side), F32),
            pltpu.VMEM((2, batch_total, 8, side), F32),
            pltpu.SMEM((2, 8, 128), jnp.int32),
            pltpu.VMEM((2, batch_total, side), F32),
            pltpu.VMEM((group_count, batch_total), jnp.int32),
        ),
        in_specs=[scalars] + [main] * 5,
        out_specs=(vector,) * 4 + (scalars,) + (vector,) * 2,
        scratch_shapes=[
            pltpu.VMEM((group_count, k_blocks, side, side), BF16),
            pltpu.VMEM((batch_total, r_groups + 1, side, side), BF16),
            pltpu.VMEM((2,) + lists.shape, jnp.int32),
            pltpu.VMEM((8, 128), jnp.int32),
            pltpu.VMEM((2, 8, 128), jnp.int32),
            pltpu.VMEM(weights.shape, BF16),
            pltpu.VMEM(relevant.shape, jnp.int32),
            pltpu.SMEM(relevant.shape, jnp.int32),
            pltpu.SMEM(lists.shape, jnp.int32),
            pltpu.SMEM((8, 128), jnp.int32),
            pltpu.SMEM((2,) + lists.shape, jnp.int32),
            dma((3,)),
            dma((4,)),
            dma((REACH,)),
            dma((REACH,)),
            dma,
            dma,
            dma,
            dma,
            dma((4,)),
            dma((4,)),
        ],
        compiler_params=pltpu.CompilerParams(
            collective_id=0, has_side_effects=True, vmem_limit_bytes=10 * MIB
        ),
        name="halo",
    )(
        live, in_hbm(relevant), in_hbm(lists), in_hbm(weights),
        in_hbm(density_blocks), in_hbm(basis_values),
    )


def edge_kernel(
    table, weights, halo, values, density_owned, start, edge_sums, density, parts, edge_total,
    part_at, edge_list,
):
    batch_total = density.shape[1]
    pages = values.shape[0] // (2 * batch_total)
    r_groups = pages - 1
    k_blocks = halo.shape[1]
    lanes = table.shape[2]
    side_row = k_blocks + lax.axis_index("rep")
    part_at[...] = jnp.zeros(part_at.shape, F32)
    del start

    found = 0
    for core in range(2):

        def collect(b, found):
            for i in range(r_groups):
                code = b * r_groups + i
                edge_list[found] = code + core * lanes
                found = found + (table[core, side_row, code] >= 0).astype(jnp.int32)
            return found

        found = lax.fori_loop(0, table[core, k_blocks + 2, 0], collect, found)
    edge_list[found] = batch_total * r_groups

    def entry(index):
        listed = edge_list[index]
        core = lax.shift_right_logical(listed, 7)
        code = listed & (lanes - 1)
        batch = core * batch_total + lax.shift_right_logical(code, 3)
        page = batch * pages
        picks = [page + table[core, k, code] for k in range(k_blocks)]
        return batch, page + (code & (r_groups - 1)), table[core, side_row, code], picks

    def for_entries(body):
        def wide(index, carry):
            body([entry(WIDE * index + n) for n in range(WIDE)])
            return carry

        wide_steps = lax.shift_right_logical(found, WIDE.bit_length() - 1)
        lax.fori_loop(0, wide_steps, wide, 0)

        def narrow(index, carry):
            body([entry(WIDE * wide_steps + 2 * index + n) for n in range(2)])
            return carry

        lax.fori_loop(0, lax.shift_right_logical(found - WIDE * wide_steps + 1, 1), narrow, 0)

    def add_density(entries):
        sums = []
        for batch, own_page, row, picks in entries:
            spread = None
            for k in range(0, k_blocks, 2):
                left_side = jnp.concatenate([halo[row, k], halo[row, k + 1]], axis=1)
                right_side = jnp.concatenate([values[picks[k]], values[picks[k + 1]]], axis=0)
                term = jnp.dot(left_side, right_side, preferred_element_type=F32)
                spread = term if spread is None else spread + term
            product = values[own_page].astype(F32) * spread
            sums.append(jnp.sum(product.reshape(-1, 8, product.shape[-1]), axis=0))
        for (batch, _, _, _), part in zip(entries, sums):
            part_at[batch] += part

    for_entries(add_density)
    factor = part_at
    for core in range(2):
        slots = pl.ds(core * batch_total, batch_total)
        part = jnp.sum(part_at[slots], axis=1)
        whole = jnp.sum(density_owned[core], axis=1) + part
        parts[core] = part
        density[core] = whole
        scale = weights[core] * potential(whole)
        factor[slots] = jnp.broadcast_to(scale[:, None, :], (batch_total,) + factor.shape[1:])

    def add_terms(entries):
        terms = []
        for batch, own_page, row, picks in entries:
            factor_row = factor[batch, 0:1, :]
            for k in range(0, k_blocks, 2):
                columns = jnp.concatenate(
                    [(values[picks[k + n]].astype(F32) * factor_row).astype(BF16) for n in range(2)],
                    axis=0,
                )
                terms.append(
                    lax.dot_general(
                        values[own_page], columns, (((1,), (1,)), ((), ())), preferred_element_type=F32
                    )
                )
        side = halo.shape[-1]
        for n, (_, _, row, _) in enumerate(entries):
            for k in range(k_blocks):
                pair = terms[n * (k_blocks // 2) + k // 2]
                edge_total[row, k] += pair[:, side * (k % 2) : side * (k % 2 + 1)]

    for_entries(add_terms)

    def pack(row):
        edge_sums[row] = edge_total[row].astype(BF16)

    each(REACH, pack)


def edge_work(fetched):
    halo, values, start, density_owned, table, weights, _ = fetched
    _, batch_total, pages, side, _ = values.shape
    flat = values.reshape(2 * batch_total * pages, side, side)
    scalars = pl.BlockSpec(memory_space=pltpu.SMEM)
    vector = pl.BlockSpec(memory_space=pltpu.VMEM)
    rows = pltpu.VMEM((2, batch_total, side), F32)
    edge_sums, density, parts, _ = pl.pallas_call(
        edge_kernel,
        out_shape=(pltpu.VMEM(halo.shape, BF16), rows, rows, pltpu.VMEM(start.shape, F32)),
        in_specs=[scalars] + [vector] * 5,
        out_specs=(vector,) * 4,
        input_output_aliases={5: 3},
        scratch_shapes=[
            pltpu.VMEM((2 * batch_total, 8, side), F32),
            pltpu.SMEM((256,), jnp.int32),
        ],
        compiler_params=pltpu.CompilerParams(vmem_limit_bytes=4 * MIB),
        name="edges",
    )(
        table, in_vmem(weights), in_vmem(halo), in_vmem(flat), in_vmem(density_owned), in_vmem(start)
    )
    return edge_sums, density, parts


def reduce_kernel(
    edge_sums, density, parts, weights, values, table_scalars, sources, out,
    factor, source_scalars, terms, scaled_even, scaled_odd, sent, got, owned, edge_in, part_in,
    small_sem, swap_send, swap_recv, edge_send, edge_recv, done_send, done_recv, part_send, part_recv,
):
    rep, faces, facing, partner = surroundings()
    group_count, k_blocks = out.shape[:2]
    batch_total, pages = values.shape[1:3]
    r_groups = pages - 1
    inner = (group_count - 2 * REACH) // 2
    announce(faces, facing, partner)
    sources_down = pltpu.make_async_copy(sources, source_scalars, small_sem.at[0])
    sources_down.start()
    blank = jnp.zeros(values.shape[3:], BF16)
    for scaled in (scaled_even, scaled_odd):
        scaled[r_groups] = blank
    terms[batch_total * r_groups] = jnp.zeros(terms.shape[1:], F32)
    edges = [
        remote(
            edge_sums.at[step, pl.ds(k, k_blocks // 2)],
            edge_in.at[step, pl.ds(k, k_blocks // 2)],
            edge_send.at[step, k // (k_blocks // 2)],
            edge_recv.at[step, k // (k_blocks // 2)],
            facing,
        )
        for step in range(REACH)
        for k in range(0, k_blocks, k_blocks // 2)
    ]
    part_move = remote(parts.at[1 - rep], part_in, part_send, part_recv, partner)
    gather_round(faces)

    @pl.when(faces)
    def _():
        for edge in edges:
            edge.start()

    part_move.start()
    sources_down.wait()

    part_move.wait_recv()
    factor[...] = weights[rep] * potential(density[rep] + part_in[...])

    def edge_at(which):
        return which * (group_count - REACH)

    def inner_at(which):
        return REACH + which * inner

    def scale(b, scaled):
        row = factor[pl.ds(b, 1), :]
        for i in range(r_groups):
            scaled[i] = (values[rep, b, i].astype(F32) * row).astype(BF16)

    def make_terms(b, scaled):
        for i in range(r_groups):
            code = b * r_groups + i
            for k in range(0, k_blocks, 2):
                columns = jnp.concatenate(
                    [scaled[table_scalars[rep, k, code]], scaled[table_scalars[rep, k + 1, code]]], axis=0
                )
                pair = lax.dot_general(
                    values[rep, b, i], columns, (((1,), (1,)), ((), ())), preferred_element_type=F32
                )
                side = pair.shape[0]
                terms[code, k] = pair[:, :side]
                terms[code, k + 1] = pair[:, side:]

    def two_batches(step):
        scale(2 * step, scaled_even)
        scale(2 * step + 1, scaled_odd)
        make_terms(2 * step, scaled_even)
        make_terms(2 * step + 1, scaled_odd)

    each(batch_total // 2, two_batches)

    def row_sum(row, k):
        held = terms[source_scalars[row, 0], k]
        for b in range(1, batch_total):
            held = held + terms[source_scalars[row, b], k]
        return held

    swaps = []

    def pack(first, at, size):
        def step(row):
            for k in range(k_blocks):
                sent[at + row, k] = row_sum(first + row, k).astype(BF16)

        each(size, step)
        index = len(swaps)
        rows_at = pl.ds(at, size)
        copy = remote(
            sent.at[rows_at], got.at[rows_at], swap_send.at[index], swap_recv.at[index], partner
        )
        copy.start()
        swaps.append(copy)

    half_inner = inner // 2
    pack(inner_at(1 - rep), REACH, half_inner)
    pack(inner_at(1 - rep) + half_inner, REACH + half_inner, half_inner)
    pack(edge_at(1 - rep), 0, REACH)

    finals = []

    def hand_over(part):
        index = len(finals)
        copy = remote(out.at[part], out.at[part], done_send.at[index], done_recv.at[index], partner)
        copy.start()
        finals.append(copy)

    for half in range(2):
        swaps[half].wait_recv()
        first = inner_at(rep) + half * half_inner
        at = REACH + half * half_inner

        def add_inner(row, first=first, at=at):
            for k in range(k_blocks):
                out[first + row, k] = (row_sum(first + row, k) + got[at + row, k].astype(F32)).astype(BF16)

        each(half_inner, add_inner)
        hand_over(pl.ds(first, half_inner))

    swaps[2].wait_recv()

    def add_owned(row):
        for k in range(k_blocks):
            owned[row, k] = row_sum(edge_at(rep) + row, k) + got[row, k].astype(F32)

    each(REACH, add_owned)
    for index, edge in enumerate(edges):
        step, blocks = index // 2, pl.ds((index % 2) * (k_blocks // 2), k_blocks // 2)
        row = edge_at(rep) + step

        @pl.when(faces)
        def _():
            edge.wait_recv()
            out[row, blocks] = (owned[step, blocks] + edge_in[step, blocks].astype(F32)).astype(BF16)

        @pl.when(jnp.logical_not(faces))
        def _():
            out[row, blocks] = owned[step, blocks].astype(BF16)

        hand_over((row, blocks))

    @pl.when(faces)
    def _():
        for edge in edges:
            edge.wait_send()

    part_move.wait_send()
    for copy in swaps:
        copy.wait_send()
    for copy in finals:
        copy.wait()


def reduced(edge_sums, density, parts, fetched):
    _, values, _, _, table, weights, sources = fetched
    group_count, batch_total = sources.shape
    k_blocks, side, _ = edge_sums.shape[1:]
    pages = values.shape[2]
    half_rows = group_count // 2
    vector = pl.BlockSpec(memory_space=pltpu.VMEM)
    dma = pltpu.SemaphoreType.DMA
    return pl.pallas_call(
        reduce_kernel,
        out_shape=pltpu.VMEM((group_count, k_blocks, side, side), BF16),
        in_specs=[vector] * 5 + [pl.BlockSpec(memory_space=pltpu.SMEM), vector],
        out_specs=vector,
        scratch_shapes=[
            pltpu.VMEM((batch_total, side), F32),
            pltpu.SMEM(sources.shape, jnp.int32),
            pltpu.VMEM((batch_total * (pages - 1) + 1, k_blocks, side, side), F32),
            pltpu.VMEM((pages, side, side), BF16),
            pltpu.VMEM((pages, side, side), BF16),
            pltpu.VMEM((half_rows, k_blocks, side, side), BF16),
            pltpu.VMEM((half_rows, k_blocks, side, side), BF16),
            pltpu.VMEM((REACH, k_blocks, side, side), F32),
            pltpu.VMEM((REACH, k_blocks, side, side), BF16),
            pltpu.VMEM((batch_total, side), F32),
            dma((1,)),
            dma((3,)),
            dma((3,)),
            dma((REACH, 2)),
            dma((REACH, 2)),
            dma((2 * REACH + 2,)),
            dma((2 * REACH + 2,)),
            dma,
            dma,
        ],
        compiler_params=pltpu.CompilerParams(
            collective_id=1, has_side_effects=True, vmem_limit_bytes=40 * MIB
        ),
        name="reduce",
    )(
        *[in_vmem(array) for array in (edge_sums, density, parts, weights, values)],
        table,
        in_vmem(sources),
    )


def shards(density_blocks, neighbours, relevant, batch_count, basis_values, becke_weights):
    fetched = fetch_halo(
        batch_count, relevant.T, neighbours.T, becke_weights, density_blocks, basis_values
    )
    edge_sums, density, parts = edge_work(fetched)
    return reduced(edge_sums, density, parts, fetched)


def solution(mesh):
    placed = (
        P("grid", None, None, None),
        P("grid", None),
        P(("grid", "rep"), None),
        P(("grid", "rep")),
        P(("grid", "rep"), None, None, None),
        P(("grid", "rep"), None),
    )
    return jax.shard_map(
        shards, mesh=mesh, in_specs=placed, out_specs=P("grid", None, None, None), check_vma=False
    )
```
